256 devices in a mesh: seq: 64 (over z, y, core), head: 4 (over x).
Axes of the slice: x: 4, y: 4, z: 8, core: 2. Of those that a mesh axis runs over, the one named last changes fastest.
Arguments:
- tokens: bfloat16 [16384, 4096], P('seq', 'head'), may hold values from -6 to 6
- light_input: bfloat16 [3, 4096, 1024], P(None, None, 'head'), may hold values from -14 to 14
- light_output: bfloat16 [1024, 4096], P('head'), may hold values from -0.75 to 0.75
- heavy_input: bfloat16 [3, 4096, 4096], P(None, 'seq', 'head'), may hold values from -14 to 14
- heavy_output: bfloat16 [4096, 4096], P('head', 'seq'), may hold values from -0.75 to 0.75
- query_tokens: int32 [64, 32], replicated, may hold values from -1 to 255, as said below
- context_tokens: int32 [64, 32], replicated, may hold values from -1 to 255, as said below
- query_gate: float32 [64, 32], P('seq'), may hold values from 0.25 to 2
Outputs:
- mixed: bfloat16 [16384, 4096], P('seq', 'head')
The draws below stay inside these ranges and needn't reach their ends.
Inputs may be any that keep to these rules, and one draw needn't show every extreme that they name: `query_tokens`: row s lists, in its first entries, distinct positions within sequence shard s of routed query tokens, and -1 after them; 512 positions are listed over all rows, at most 32 in a row, and exactly 32 in some row. `context_tokens`: row s lists, in its first entries, distinct positions within sequence shard s of routed key-value tokens, and -1 after them; 512 positions are listed over all rows, at most 32 in a row, and exactly 32 in some row.
All inputs are finite; a program needn't handle non-finite values.
Results may differ from the reference program's by a relative error of at most 0.012.
Values may be sent and summed in bfloat16 or wider, within the bound.
A program may use at most 64 MiB of HBM per device.

```python
import math
import jax
import jax.numpy as jnp
from jax import lax

TOK_DEV = 256
D = 4096
HD = 128
LH = 8
HH = 32
LB = 128
LW = 1024
HW = 4096
CQ = 32
TOKENS = 16384
ROUTED = 512
N_SEQ = 64


def shard_places(subkey):
    return jax.random.permutation(subkey, TOK_DEV)[:CQ]


def route_table(key, salt):
    streams = jax.random.split(jax.random.fold_in(key, salt), 5)
    shard_total = TOKENS // TOK_DEV
    groups = shard_total // 4
    first_count = jax.random.randint(streams[0], (groups,), 0, CQ // 2 + 1)
    second_count = jax.random.randint(streams[1], (groups,), 0, (CQ - first_count) // 2 + 1)
    third_count = jax.random.randint(streams[2], (groups,), 0, (CQ - first_count - second_count) // 2 + 1)
    leading = jnp.arange(groups) == 0
    first_count = jnp.where(leading, 0, first_count)
    second_count = jnp.where(leading, 0, second_count)
    third_count = jnp.where(leading, 0, third_count)
    fourth_count = CQ - first_count - second_count - third_count
    counts = jnp.stack([first_count, second_count, third_count, fourth_count], axis=1).reshape(shard_total)
    counts = jnp.take(counts, jax.random.permutation(streams[3], shard_total))
    places = jax.vmap(shard_places)(jax.random.split(streams[4], shard_total))
    position = jnp.arange(CQ)[None, :]
    return jnp.where(position < counts[:, None], places, -1).astype(jnp.int32)


def drawn_weights(key, salt, width):
    streams = jax.random.split(jax.random.fold_in(key, salt), 1)
    fan_scale = 1.0 / math.sqrt(D)
    return jnp.clip(jax.random.normal(streams[0], (3, D, width), jnp.float32), -6.0, 6.0) * fan_scale


def draw_tokens(key, part):
    streams = jax.random.split(jax.random.fold_in(key, 5), 1)
    return jnp.clip(jax.random.normal(streams[0], (TOKENS, D), jnp.float32), -6.0, 6.0).astype(jnp.bfloat16)


def draw_light_input(key, part):
    return drawn_weights(key, 3, LH * HD).astype(jnp.bfloat16)


def draw_heavy_input(key, part):
    return drawn_weights(key, 4, HH * HD).astype(jnp.bfloat16)


def draw_query_tokens(key, part):
    return route_table(key, 11)


def draw_context_tokens(key, part):
    return route_table(key, 23)


def shard_levels(own_key, shape, shards, least, high):
    gain, own = 1.0, jax.random.fold_in(own_key, 6)
    for dim, parts in shards:
        draws = jnp.exp(jax.random.uniform(jax.random.fold_in(own, dim), (parts,), jnp.float32, least / len(shards), high / len(shards)))
        gain = gain * jnp.repeat(draws, shape[dim] // parts).reshape([-1 if axis == dim else 1 for axis in range(len(shape))])
    return gain


def normal_values(key, extent, deviation, reach, cuts=(), kind=jnp.bfloat16):
    entries = jax.random.normal(key, extent, jnp.float32) * deviation
    if len(cuts) > 0:
        entries = shard_levels(key, extent, cuts, -0.22, 0.18) * entries
    return jnp.clip(entries, min=-reach, max=reach).astype(kind)


def setup_inputs(seed: int = 0) -> dict:
    keys = jax.random.split(jax.random.key(seed), 9)
    return {
        "tokens": draw_tokens(jax.random.fold_in(keys[8], 71), 0),
        "light_input": draw_light_input(jax.random.fold_in(keys[8], 71), 0),
        "light_output": normal_values(keys[2], (LW, D), (LW // 16) ** -0.5, 0.75, ((0, 4),)),
        "heavy_input": draw_heavy_input(jax.random.fold_in(keys[8], 71), 0),
        "heavy_output": normal_values(keys[4], (HW, D), (HW // 64) ** -0.5, 0.75, ((0, 4), (1, 64))),
        "query_tokens": draw_query_tokens(jax.random.fold_in(keys[8], 71), 0),
        "context_tokens": draw_context_tokens(jax.random.fold_in(keys[8], 71), 0),
        "query_gate": jnp.clip(jnp.exp(math.log(2.0) - 2.0794415 * jax.random.uniform(keys[7], (N_SEQ, CQ), jnp.float32) ** shard_levels(keys[7], (N_SEQ, CQ), ((0, 64),), -0.2, 0.2)), 0.25, 2.0),
    }


def attend(queries, key_rows, value_rows):
    scores = jnp.einsum('bqhe,bkhe->bhqk', queries.astype(jnp.float32), key_rows.astype(jnp.float32)) / math.sqrt(queries.shape[-1])
    highest = lax.optimization_barrier(jnp.max(scores, axis=-1, keepdims=True))
    expanded = jnp.exp(scores - highest)
    totals = lax.optimization_barrier(jnp.sum(expanded, axis=-1))
    rounded = lax.optimization_barrier(expanded.astype(jnp.bfloat16))
    weighted = jnp.einsum('bhqk,bkhe->bqhe', rounded.astype(jnp.float32), value_rows.astype(jnp.float32))
    return (weighted / jnp.transpose(totals, (0, 2, 1))[..., None]).astype(jnp.bfloat16)

def routed_list(table):
    counts = lax.optimization_barrier(jnp.sum((table >= 0).astype(jnp.int32), axis=1))
    upper_end = jnp.cumsum(counts).astype(jnp.int32)
    lower_end = (upper_end - counts).astype(jnp.int32)
    compact_rows = jnp.arange(ROUTED, dtype=jnp.int32)
    source_shard = lax.optimization_barrier(jnp.sum((upper_end[None, :] <= compact_rows[:, None]).astype(jnp.int32), axis=1)).astype(jnp.int32)
    within = (compact_rows - lower_end[source_shard]).astype(jnp.int32)
    positions = (source_shard * TOK_DEV + table[source_shard, within]).astype(jnp.int32)
    return (source_shard, within, positions)

def reference(tokens, light_input, light_output, heavy_input, heavy_output, query_tokens, context_tokens, query_gate):
    light_mapped = jnp.stack([jnp.dot(tokens, light_input[c], preferred_element_type=jnp.float32).astype(jnp.bfloat16) for c in range(3)])
    light_blocks = light_mapped.reshape(3, TOKENS // LB, LB, LH, HD)
    light_heads = attend(light_blocks[0], light_blocks[1], light_blocks[2]).reshape(TOKENS, LH * HD)
    light_update = jnp.dot(light_heads, light_output, preferred_element_type=jnp.float32)
    query_shard, query_within, query_list = routed_list(query_tokens)
    context_list = routed_list(context_tokens)[2]
    query_rows = tokens[query_list]
    context_rows = tokens[context_list]
    heavy_queries = jnp.dot(query_rows, heavy_input[0], preferred_element_type=jnp.float32).astype(jnp.bfloat16)
    heavy_keys = jnp.dot(context_rows, heavy_input[1], preferred_element_type=jnp.float32).astype(jnp.bfloat16)
    heavy_values = jnp.dot(context_rows, heavy_input[2], preferred_element_type=jnp.float32).astype(jnp.bfloat16)
    heavy_heads = attend(heavy_queries.reshape(1, ROUTED, HH, HD), heavy_keys.reshape(1, ROUTED, HH, HD), heavy_values.reshape(1, ROUTED, HH, HD)).reshape(ROUTED, HH * HD)
    heavy_update = jnp.dot(heavy_heads, heavy_output, preferred_element_type=jnp.float32)
    gate_values = query_gate[query_shard, query_within]
    mixed = light_update.at[query_list].add(gate_values[:, None] * heavy_update)
    return mixed.astype(jnp.bfloat16)
```

```python
import functools
import math

import jax
import jax.numpy as jnp
from jax import lax
from jax.experimental import pallas as pl
from jax.experimental.pallas import tpu as pltpu
from jax.sharding import PartitionSpec as P

HD = 128
LB = 128
FB = 128
BF = jnp.bfloat16
F32 = jnp.float32


def dot(a, b):
    return jnp.dot(a, b, preferred_element_type=F32)


def dot_nt(a, b):
    return lax.dot_general(a, b, (((1,), (1,)), ((), ())), preferred_element_type=F32)


def iota(shape, dim):
    return lax.broadcasted_iota(jnp.int32, shape, dim)


def as_column(row):
    n = row.shape[1]
    wide = jnp.broadcast_to(row, (n, n))
    return jnp.sum(jnp.where(iota((n, n), 0) == iota((n, n), 1), wide, 0.0), axis=1, keepdims=True)


def onehot(hit):
    return jnp.where(hit, 1.0, 0.0).astype(BF)


def compact_index(table):
    shards, slots = table.shape
    per = 128 // slots
    rows = shards // per
    spread = onehot(iota((slots, 128), 1) % slots == iota((slots, 128), 0))
    tiled = dot(table.astype(F32).astype(BF), spread)
    keep = iota((shards, 128), 0) % per == iota((shards, 128), 1) // slots
    join = onehot(iota((rows, shards), 1) // per == iota((rows, shards), 0))
    flat = dot(join, jnp.where(keep, tiled, 0.0).astype(BF))
    live = flat >= 0.0
    marks = onehot(live)
    before = dot(marks, onehot(iota((128, 128), 0) < iota((128, 128), 1)))
    in_row = dot(marks, jnp.ones((128, 128), BF))
    above = dot(onehot(iota((rows, rows), 1) < iota((rows, rows), 0)), in_row.astype(BF))
    return jnp.where(live, before + above, -1.0)


def softmax_value(q, k, v):
    scores = dot_nt(q, k) * (1.0 / math.sqrt(HD))
    expanded = jnp.exp(scores - jnp.max(scores, axis=-1, keepdims=True))
    totals = jnp.sum(expanded, axis=-1, keepdims=True)
    return (dot(expanded.astype(BF), v) / totals).astype(BF)


def kernel(
    dims,
    tok, lin, lout, hin, hout, qtab, ctab, gate,
    out,
    picks, landed, comp, sel, xall, wbuf, part, rsum, kv, qbuf, oz, oy,
    wother, wcat, rmine, rother, rsel, ret,
    tall, lw, lo, lmap, lheads, lsend, lrecv, lacc, cidx,
    s1s, s1r, wss, wsr, wos, wor, tks, tkr, xs, xr, rs, rr, kvs, kvr, qs, qr,
    ozs, ozr, oys, oyr, cs, cr, rts, rtr, lrs, lrr, lis, los, self1, self2, self3, self4,
):
    Z, Y, X = dims
    nb = 2 * Y
    S = Z * Y * 2
    R = comp.shape[0]
    rz = R // Z
    slots = qtab.shape[1]
    T = tok.shape[0]
    FX = tok.shape[1]
    s = lax.axis_index("seq")
    x = lax.axis_index("head")
    z = s // (2 * Y)
    y = (s // 2) % Y
    c = s % 2

    def seq_of(zz, yy, cc):
        return (zz * Y + yy) * 2 + cc

    def send(src, dst, ss, rsem, to):
        pltpu.make_async_remote_copy(
            src_ref=src, dst_ref=dst, send_sem=ss, recv_sem=rsem,
            device_id=to, device_id_type=pl.DeviceIdType.MESH,
        ).start()

    def drain(ref, sem):
        pltpu.make_async_copy(ref, ref, sem).wait()

    load_in = pltpu.make_async_copy(lin, lw, lis)
    load_out = pltpu.make_async_copy(lout, lo, los)
    load_in.start()
    load_out.start()

    own_q = qtab[pl.ds(s, 1), :].astype(F32)
    own_c = ctab[pl.ds(s, 1), :].astype(F32)
    for i, row in enumerate((own_q, own_c)):
        want = onehot(as_column(row) == iota((slots, T), 1).astype(F32))
        rows = dot(want, tok[...]).astype(BF)
        for b in range(nb):
            picks[i, b] = rows[:, b * FB:(b + 1) * FB]

    handler = z // 2 == x
    own_block = (z % 2) * Y + y
    fan = nb * X * 2

    def route(i, _):
        n = lax.rem(i + s, fan)
        b = n // (2 * X)
        xt = (n // 2) % X
        ct = n % 2
        st = seq_of(2 * x + b // Y, b % Y, ct)
        here = jnp.logical_and(st == s, xt == x)

        @pl.when(jnp.logical_not(here))
        def _():
            send(picks.at[ct, b], landed.at[s], s1s, s1r, (st, xt))

        return 0

    lax.fori_loop(0, fan, route, 0)

    @pl.when(handler)
    def _():
        landed[pl.ds(s, 1)] = picks[pl.ds(c, 1), pl.ds(own_block, 1)].reshape(1, slots, FB)

    j = 2 * y + c

    def weights_out(i, _):
        jt = lax.rem(j + 1 + i, nb)
        yt = jt // 2
        ct = jt % 2
        cols = pl.ds(pl.multiple_of(yt * 2 * HD, 2 * HD), 2 * HD)

        @pl.when(ct == 0)
        def _():
            send(hin.at[pl.ds(0, 1), :, cols], wbuf.at[pl.ds(0, 1), j], wss, wsr, (seq_of(z, yt, ct), x))

        @pl.when(ct == 1)
        def _():
            send(hin.at[pl.ds(1, 2), :, cols], wbuf.at[pl.ds(0, 2), j], wss, wsr, (seq_of(z, yt, ct), x))

        return 0

    lax.fori_loop(0, nb - 1, weights_out, 0)
    own_cols = pl.ds(pl.multiple_of(y * 2 * HD, 2 * HD), 2 * HD)

    @pl.when(c == 0)
    def _():
        wbuf[pl.ds(0, 1), pl.ds(j, 1)] = hin[pl.ds(0, 1), :, own_cols].reshape(1, 1, hin.shape[1], 2 * HD)

    @pl.when(c == 1)
    def _():
        wbuf[pl.ds(0, 2), pl.ds(j, 1)] = hin[pl.ds(1, 2), :, own_cols].reshape(2, 1, hin.shape[1], 2 * HD)

    twin = (seq_of(z, y, 1 - c), x)
    send(hout.at[:, 1 - c], wother, wos, wor, twin)

    for d in range(1, X):
        send(tok, tall.at[x], tks.at[d], tkr.at[d], (s, lax.rem(x + d, X)))

    q_idx = compact_index(qtab[...])
    c_idx = compact_index(ctab[...])
    mine = jnp.where(c == 0, q_idx, c_idx)
    krows = mine.shape[0]
    row_id = iota((R, 128), 0).astype(F32)
    for k in range(krows):
        comp[:, k * 128:(k + 1) * 128] = onehot(row_id == mine[k:k + 1, :])
    cidx[...] = q_idx
    half = krows // 2
    col_id = iota((128, R), 1).astype(F32)
    for k in range(half):
        column = as_column(cidx[pl.ds(half * c + k, 1), :])
        sel[k * 128:(k + 1) * 128, :] = onehot(column == col_id)

    @pl.when(handler)
    def _():
        drain(landed.at[pl.ds(0, S - 1)], s1r)

    @pl.when(jnp.logical_not(handler))
    def _():
        drain(landed, s1r)

    xall[pl.ds(y, 1)] = dot(comp[...], landed[...].reshape(S * slots, FB)).astype(BF).reshape(1, R, FB)
    for d in range(1, Y):
        send(xall.at[y], xall.at[y], xs, xr, (seq_of(z, lax.rem(y + d, Y), c), x))

    drain(wother, wor)
    place = iota((FB // 2, FB), 1) - iota((FB // 2, FB), 0)
    mine_w = hout[:, pl.ds(c, 1)].reshape(Y * HD, FB // 2)
    their_w = wother[...].reshape(Y * HD, FB // 2)
    wcat[...] = (
        dot(mine_w, onehot(place == (FB // 2) * c)) + dot(their_w, onehot(place == (FB // 2) * (1 - c)))
    ).astype(BF)

    @pl.when(c == 0)
    def _():
        drain(wbuf.at[pl.ds(0, 1), pl.ds(0, nb - 1)], wsr)

    @pl.when(c == 1)
    def _():
        drain(wbuf.at[pl.ds(0, 2), pl.ds(0, nb - 1)], wsr)

    if Y > 1:
        drain(xall.at[pl.ds(0, Y - 1)], xr)

    def projected(i):
        total = None
        for yy in range(Y):
            term = dot(xall[yy], wbuf[i, 2 * yy:2 * yy + 2].reshape(FB, 2 * HD))
            total = term if total is None else total + term
        part[:, i] = total.astype(BF).reshape(Z, rz, 2 * HD)

    projected(0)

    @pl.when(c == 1)
    def _():
        projected(1)

    def sum_out(i, _):
        zt = lax.rem(z + 1 + i, Z)

        @pl.when(c == 0)
        def _():
            send(part.at[zt, pl.ds(0, 1)], rsum.at[z, pl.ds(0, 1)], rs, rr, (seq_of(zt, y, c), x))

        @pl.when(c == 1)
        def _():
            send(part.at[zt], rsum.at[z], rs, rr, (seq_of(zt, y, c), x))

        return 0

    lax.fori_loop(0, Z - 1, sum_out, 0)
    rsum[pl.ds(z, 1), 0:1] = part[pl.ds(z, 1), 0:1]

    @pl.when(c == 1)
    def _():
        rsum[pl.ds(z, 1), 1:2] = part[pl.ds(z, 1), 1:2]

    load_in.wait()

    def project_light(source, at, first):
        def one(i, _):
            term = dot(source[...], lw[i, pl.ds(pl.multiple_of(at * FX, FX), FX), :])
            if first:
                lmap[i] = term
            else:
                lmap[i] += term
            return 0

        lax.fori_loop(0, 3, one, 0)

    project_light(tok, x, True)

    @pl.when(c == 0)
    def _():
        drain(rsum.at[pl.ds(0, Z - 1), pl.ds(0, 1)], rr)
        rows = jnp.sum(rsum[:, 0].astype(F32), axis=0).astype(BF)
        qbuf[0] = rows[:, :HD]
        qbuf[1] = rows[:, HD:]
        send(qbuf.at[1], qbuf.at[0], qs, qr, twin)

    @pl.when(c == 1)
    def _():
        drain(rsum.at[pl.ds(0, Z - 1)], rr)
        for i in range(2):
            rows = jnp.sum(rsum[:, i].astype(F32), axis=0).astype(BF)
            for g in range(2):
                kv[g, i, pl.ds(z, 1)] = rows[:, g * HD:(g + 1) * HD].reshape(1, rz, HD)

        def kv_zero(i, _):
            zt = lax.rem(z + i, Z)
            send(kv.at[0, :, z], kv.at[1, :, z], kvs, kvr, (seq_of(zt, y, 0), x))
            return 0

        def kv_one(i, _):
            zt = lax.rem(z + 1 + i, Z)
            send(kv.at[1, :, z], kv.at[1, :, z], kvs, kvr, (seq_of(zt, y, 1), x))
            return 0

        lax.fori_loop(0, Z, kv_zero, 0)
        lax.fori_loop(0, Z - 1, kv_one, 0)

    for d in range(1, X):
        src = lax.rem(x + X - d, X)
        drain(tall.at[0], tkr.at[d])
        project_light(tall.at[src], src, False)

    @pl.when(c == 0)
    def _():
        drain(kv.at[1], kvr)

    @pl.when(c == 1)
    def _():
        drain(qbuf.at[0], qr)
        drain(kv.at[1, :, pl.ds(0, Z - 1)], kvr)

    heads = softmax_value(qbuf[0], kv[1, 0].reshape(R, HD), kv[1, 1].reshape(R, HD))
    oz[pl.ds(z, 1)] = heads.reshape(1, rz, HD)

    def heads_out(i, _):
        zt = lax.rem(z + 1 + i, Z)
        send(oz.at[z], oz.at[z], ozs, ozr, (seq_of(zt, y, c), x))
        return 0

    lax.fori_loop(0, Z - 1, heads_out, 0)

    for g in range(2):
        for blk in range(T // LB):
            rows = slice(blk * LB, (blk + 1) * LB)
            cols = slice(g * HD, (g + 1) * HD)
            lheads[rows, cols] = softmax_value(
                lmap[0, rows, cols].astype(BF), lmap[1, rows, cols].astype(BF), lmap[2, rows, cols].astype(BF)
            )
    load_out.wait()
    for d in range(1, X):
        xt = lax.rem(x + d, X)
        lsend[pl.ds(xt, 1)] = dot(
            lheads[...], lo[:, pl.ds(pl.multiple_of(xt * FX, FX), FX)]
        ).astype(BF).reshape(1, T, FX)
        send(lsend.at[xt], lrecv.at[x], lrs, lrr, (s, xt))

    drain(oz.at[pl.ds(0, Z - 1)], ozr)
    for d in range(1, Y):
        send(oz, oy.at[y], oys, oyr, (seq_of(z, lax.rem(y + d, Y), c), x))
    oy[pl.ds(y, 1)] = oz[...].reshape(1, Z, rz, HD)
    lacc[...] = dot(lheads[...], lo[:, pl.ds(pl.multiple_of(x * FX, FX), FX)])

    if Y > 1:
        drain(oy.at[pl.ds(0, Y - 1)], oyr)
    total = None
    for yy in range(Y):
        term = dot(oy[yy].reshape(R, HD), wcat[yy * HD:(yy + 1) * HD, :])
        total = term if total is None else total + term
    rmine[...] = total.astype(BF)
    send(rmine, rother, cs, cr, twin)
    drain(rother, cr)
    both = (total + rother[...].astype(F32)).astype(BF)
    rsel[...] = dot(sel[...], both).astype(BF).reshape(S // 2, slots, FB)

    block = pl.ds(pl.multiple_of(own_block * FB, FB), FB)
    xq = z // 2

    def give(i, _):
        n = lax.rem(i + s + x * Y, S // 2)
        st = (S // 2) * c + n
        here = jnp.logical_and(st == s, xq == x)

        @pl.when(jnp.logical_not(here))
        def _():
            send(rsel.at[n], ret.at[x, :, block], rts, rtr, (st, xq))

        return 0

    lax.fori_loop(0, S // 2, give, 0)
    keeps = jnp.logical_and(handler, s // (S // 2) == c)

    @pl.when(keeps)
    def _():
        ret[pl.ds(x, 1), :, block] = rsel[pl.ds(lax.rem(s, S // 2), 1)]

    if X > 1:
        drain(lrecv.at[pl.ds(0, X - 1)], lrr)
    light = lacc[...]
    for d in range(1, X):
        light = light + lrecv[pl.ds(lax.rem(x + d, X), 1)].reshape(T, FX).astype(F32)
    lacc[...] = light
    onto = onehot(own_q == iota((T, slots), 0).astype(F32))
    gates = as_column(gate[...])

    gets = jnp.logical_and(handler, s // (S // 2) == c)

    @pl.when(gets)
    def _():
        drain(landed.at[pl.ds(0, nb * X - 1)], rtr)

    @pl.when(jnp.logical_not(gets))
    def _():
        drain(landed.at[pl.ds(0, nb * X)], rtr)

    update = jnp.sum(ret[...].astype(F32), axis=0) * gates
    high = update.astype(BF)
    low = (update - high.astype(F32)).astype(BF)
    out[...] = (lacc[...] + dot(onto, high) + dot(onto, low)).astype(BF)

    @pl.when(handler)
    def _():
        drain(landed.at[pl.ds(0, fan - 1)], s1s)

    @pl.when(jnp.logical_not(handler))
    def _():
        drain(landed.at[pl.ds(0, fan)], s1s)

    @pl.when(c == 0)
    def _():
        drain(wbuf.at[pl.ds(0, 1), pl.ds(0, Y - 1)], wss) if Y > 1 else None
        drain(wbuf.at[pl.ds(0, 2), pl.ds(0, Y)], wss)

    @pl.when(c == 1)
    def _():
        drain(wbuf.at[pl.ds(0, 1), pl.ds(0, Y)], wss)
        drain(wbuf.at[pl.ds(0, 2), pl.ds(0, Y - 1)], wss) if Y > 1 else None

    drain(wother, wos)
    for d in range(1, X):
        drain(tall.at[0], tks.at[d])
    if Y > 1:
        drain(xall.at[pl.ds(0, Y - 1)], xs)
        drain(oy.at[pl.ds(0, Y - 1)], oys)

    @pl.when(c == 0)
    def _():
        drain(rsum.at[pl.ds(0, Z - 1), pl.ds(0, 1)], rs)
        drain(qbuf.at[0], qs)

    @pl.when(c == 1)
    def _():
        drain(rsum.at[pl.ds(0, Z - 1)], rs)
        drain(kv.at[0], kvs)
        drain(kv.at[0, :, pl.ds(0, Z - 1)], kvs)

    drain(oz.at[pl.ds(0, Z - 1)], ozs)
    drain(rmine, cs)

    @pl.when(keeps)
    def _():
        drain(rsel.at[pl.ds(0, S // 2 - 1)], rts)

    @pl.when(jnp.logical_not(keeps))
    def _():
        drain(rsel, rts)

    if X > 1:
        drain(lrecv.at[pl.ds(0, X - 1)], lrs)


def body(dims, tokens, light_input, light_output, heavy_input, heavy_output, query_tokens, context_tokens, query_gate):
    Z, Y, X = dims
    S = Z * Y * 2
    nb = 2 * Y
    slots = query_tokens.shape[1]
    T, FX = tokens.shape
    R = S * T // 32
    rz = R // Z
    D = light_input.shape[1]
    LX = light_input.shape[2]
    hout = heavy_output.reshape(Y, 2, HD, FB // 2)
    vm = pl.BlockSpec(memory_space=pltpu.VMEM)
    hbm = pl.BlockSpec(memory_space=pl.ANY)
    dma = pltpu.SemaphoreType.DMA
    scratch = [
        pltpu.VMEM((2, nb, slots, FB), BF),
        pltpu.VMEM((S, slots, FB), BF),
        pltpu.VMEM((R, S * slots), BF),
        pltpu.VMEM((S * slots // 2, R), BF),
        pltpu.VMEM((Y, R, FB), BF),
        pltpu.VMEM((2, nb, FB // 2, 2 * HD), BF),
        pltpu.VMEM((Z, 2, rz, 2 * HD), BF),
        pltpu.VMEM((Z, 2, rz, 2 * HD), BF),
        pltpu.VMEM((2, 2, Z, rz, HD), BF),
        pltpu.VMEM((2, rz, HD), BF),
        pltpu.VMEM((Z, rz, HD), BF),
        pltpu.VMEM((Y, Z, rz, HD), BF),
        pltpu.VMEM((Y, HD, FB // 2), BF),
        pltpu.VMEM((Y * HD, FB), BF),
        pltpu.VMEM((R, FB), BF),
        pltpu.VMEM((R, FB), BF),
        pltpu.VMEM((S // 2, slots, FB), BF),
        pltpu.VMEM((X, slots, FX), BF),
        pltpu.VMEM((X, T, FX), BF),
        pltpu.VMEM((3, D, LX), BF),
        pltpu.VMEM((LX, D), BF),
        pltpu.VMEM((3, T, LX), F32),
        pltpu.VMEM((T, LX), BF),
        pltpu.VMEM((X, T, FX), BF),
        pltpu.VMEM((X, T, FX), BF),
        pltpu.VMEM((T, FX), F32),
        pltpu.VMEM((S * slots // 128, 128), F32),
        dma(()), dma(()), dma(()), dma(()), dma(()), dma(()),
        dma((X,)), dma((X,)),
        *[dma(()) for _ in range(24)],
    ]
    return pl.pallas_call(
        functools.partial(kernel, dims),
        out_shape=jax.ShapeDtypeStruct((T, FX), BF),
        in_specs=[vm, hbm, hbm, vm, vm, vm, vm, vm],
        out_specs=vm,
        scratch_shapes=scratch,
        compiler_params=pltpu.CompilerParams(has_side_effects=True, vmem_limit_bytes=56 << 20),
    )(tokens, light_input, light_output, heavy_input, hout, query_tokens, context_tokens, query_gate)


def solution(mesh):
    X = mesh.shape["head"]
    Z = 2 * X
    dims = (Z, mesh.shape["seq"] // (2 * Z), X)
    placed = (
        P("seq", "head"),
        P(None, None, "head"),
        P("head", None),
        P(None, "seq", "head"),
        P("head", "seq"),
        P(),
        P(),
        P("seq", None),
    )
    return jax.shard_map(
        functools.partial(body, dims), mesh=mesh, in_specs=placed, out_specs=P("seq", "head"), check_vma=False
    )
```

```python
import functools
import math

import jax
import jax.numpy as jnp
from jax import lax
from jax.experimental import pallas as pl
from jax.experimental.pallas import tpu as pltpu
from jax.sharding import PartitionSpec as P

HD = 128
LB = 128
FB = 128
BF = jnp.bfloat16
F32 = jnp.float32


def dot(a, b):
    return jnp.dot(a, b, preferred_element_type=F32)


def dot_nt(a, b):
    return lax.dot_general(a, b, (((1,), (1,)), ((), ())), preferred_element_type=F32)


def iota(shape, dim):
    return lax.broadcasted_iota(jnp.int32, shape, dim)


def as_column(row):
    n = row.shape[1]
    wide = jnp.broadcast_to(row, (n, n))
    return jnp.sum(jnp.where(iota((n, n), 0) == iota((n, n), 1), wide, 0.0), axis=1, keepdims=True)


def as_row(column):
    n = column.shape[0]
    wide = jnp.broadcast_to(column, (n, n))
    return jnp.sum(jnp.where(iota((n, n), 0) == iota((n, n), 1), wide, 0.0), axis=0, keepdims=True)


def onehot(hit):
    return jnp.where(hit, 1.0, 0.0).astype(BF)


def compact_index(table):
    slots, shards = table.shape
    per = 128 // slots
    rows = shards // per
    spread = onehot(iota((128, slots), 0) % slots == iota((128, slots), 1))
    tiled = dot(spread, table.astype(F32).astype(BF))
    keep = iota((128, shards), 1) % per == iota((128, shards), 0) // slots
    join = onehot(iota((rows, shards), 1) // per == iota((rows, shards), 0))
    flat = dot_nt(join, jnp.where(keep, tiled, 0.0).astype(BF))
    live = flat >= 0.0
    marks = onehot(live)
    before = dot(marks, onehot(iota((128, 128), 0) < iota((128, 128), 1)))
    in_row = dot(marks, jnp.ones((128, 128), BF))
    above = dot(onehot(iota((rows, rows), 1) < iota((rows, rows), 0)), in_row.astype(BF))
    return jnp.where(live, before + above, -1.0)


def softmax_value(q, k, v):
    scores = dot_nt(q, k) * (1.0 / math.sqrt(HD))
    expanded = jnp.exp(scores - jnp.max(scores, axis=-1, keepdims=True))
    totals = jnp.sum(expanded, axis=-1, keepdims=True)
    return (dot(expanded.astype(BF), v) / totals).astype(BF)


def kernel(
    dims,
    tok_any, lin, lout, hin_any, hout_any, qtab_any, ctab_any, gate_any,
    out,
    tok, hin, hout, qtab, ctab, gate,
    picks, planes, landed, comp, sel, xall, wbuf, part, rsum, kv, qbuf, oz, oy,
    wcat, rmine, rother, rsel, ret,
    tall, lw, lo, lmap, lheads, lsend, lfar, lrecv, lacc, cidx,
    s0s, s0r, s1s, s1r, wss, wsr, wos, wor, rs, rr, kvs, kvr, qs, qr,
    ozs, ozr, oys, oyr, cs, cr, rts, rtr, lrs, lrr, lis, los,
    tks, tkr, xs, xr, lfr, ins,
):
    Z, Y, X = dims
    NY = Y // X
    nb = 2 * Y
    S = Z * Y * 2
    R = comp.shape[0]
    rz = R // Z
    slots = qtab.shape[0]
    T = tok.shape[0]
    FX = tok.shape[1]
    s = lax.axis_index("seq")
    x = lax.axis_index("head")
    z = s // (2 * Y)
    y = (s // 2) % Y
    c = s % 2
    right, left = lax.rem(x + 1, X), lax.rem(x + X - 1, X)
    far = lax.rem(x + 2, X)

    def seq_of(zz, yy, cc):
        return (zz * Y + yy) * 2 + cc

    twin = (seq_of(z, y, 1 - c), x)

    def send(src, dst, ss, rsem, to):
        pltpu.make_async_remote_copy(
            src_ref=src, dst_ref=dst, send_sem=ss, recv_sem=rsem,
            device_id=to, device_id_type=pl.DeviceIdType.MESH,
        ).start()

    def drain(ref, sem):
        pltpu.make_async_copy(ref, ref, sem).wait()

    barrier = pltpu.get_barrier_semaphore()

    def greet(to):
        pl.semaphore_signal(barrier, inc=1, device_id=to, device_id_type=pl.DeviceIdType.MESH)

    handler = y % X == x

    for d in range(1, nb):
        jt = lax.rem(2 * y + c + d, nb)
        greet((seq_of(z, jt // 2, jt % 2), x))
    for d in range(1, X):
        greet((s, lax.rem(x + d, X)))

    @pl.when(handler)
    def _():
        def greet_plane(i, _):
            greet((lax.rem(s + 1 + i, S), x))
            return 0

        lax.fori_loop(0, S - 1, greet_plane, 0)

    fetches = [
        pltpu.make_async_copy(src, dst, ins.at[i])
        for i, (src, dst) in enumerate((
            (qtab_any, qtab), (ctab_any, ctab), (tok_any, tok), (hin_any, hin), (hout_any, hout), (gate_any, gate),
        ))
    ]
    for fetch in fetches:
        fetch.start()
    load_in = pltpu.make_async_copy(lin, lw, lis)
    load_out = pltpu.make_async_copy(lout, lo, los)
    load_in.start()
    load_out.start()

    fetches[0].wait()
    fetches[1].wait()
    here_s = iota((slots, S), 1) == s
    own_q = jnp.sum(jnp.where(here_s, qtab[...].astype(F32), 0.0), axis=1, keepdims=True)
    own_c = jnp.sum(jnp.where(here_s, ctab[...].astype(F32), 0.0), axis=1, keepdims=True)
    fetches[2].wait()
    for i, column in enumerate((own_q, own_c)):
        want = onehot(column == iota((slots, T), 1).astype(F32))
        rows = dot(want, tok[...]).astype(BF)
        for b in range(nb):
            picks[b % Y, b // Y, i] = rows[:, b * FB:(b + 1) * FB]

    met = (nb - 1) + (X - 1) + NY * Z * 2

    @pl.when(handler)
    def _():
        pl.semaphore_wait(barrier, met - 1)

    @pl.when(jnp.logical_not(handler))
    def _():
        pl.semaphore_wait(barrier, met)

    for d in range(1, X):
        xt = lax.rem(x + d, X)
        for i in range(NY):
            send(picks.at[i * X + xt], planes.at[i, x], s0s, s0r, (s, xt))
    for i in range(NY):
        planes[i, pl.ds(x, 1)] = picks[pl.ds(i * X + x, 1)]

    mine_rows = pl.ds(pl.multiple_of(c * (FB // 2), FB // 2), FB // 2)
    fetches[3].wait()
    fetches[4].wait()
    fetches[5].wait()
    for yy in range(Y):
        wcat[mine_rows, yy * HD:(yy + 1) * HD] = hout[:, pl.ds(pl.multiple_of((2 * yy + c) * HD, HD), HD)]
    if X > 1:
        drain(planes.at[:, pl.ds(0, X - 1)], s0r)

    fan = NY * Z * 2

    def route(i, _):
        n = lax.rem(i + 2 * z + c, fan)
        yi = n // (2 * Z)
        zt = (n // 2) % Z
        ct = n % 2
        st = seq_of(zt, yi * X + x, ct)

        @pl.when(st != s)
        def _():
            send(planes.at[yi, zt // 2, zt % 2, ct], landed.at[s], s1s, s1r, (st, x))

        return 0

    lax.fori_loop(0, fan, route, 0)

    @pl.when(handler)
    def _():
        landed[pl.ds(s, 1)] = planes[
            pl.ds(y // X, 1), pl.ds(z // 2, 1), pl.ds(z % 2, 1), pl.ds(c, 1)
        ].reshape(1, slots, FB)

    j = 2 * y + c

    def weights_out(i, _):
        jt = lax.rem(j + 1 + i, nb)
        yt = jt // 2
        ct = jt % 2
        cols = pl.ds(pl.multiple_of(yt * 2 * HD, 2 * HD), 2 * HD)

        @pl.when(ct == 0)
        def _():
            send(hin.at[pl.ds(0, 1), :, cols], wbuf.at[pl.ds(0, 1), j], wss, wsr, (seq_of(z, yt, ct), x))

        @pl.when(ct == 1)
        def _():
            send(hin.at[pl.ds(1, 2), :, cols], wbuf.at[pl.ds(0, 2), j], wss, wsr, (seq_of(z, yt, ct), x))

        return 0

    lax.fori_loop(0, nb - 1, weights_out, 0)
    own_cols = pl.ds(pl.multiple_of(y * 2 * HD, 2 * HD), 2 * HD)

    @pl.when(c == 0)
    def _():
        wbuf[pl.ds(0, 1), pl.ds(j, 1)] = hin[pl.ds(0, 1), :, own_cols].reshape(1, 1, hin.shape[1], 2 * HD)

    @pl.when(c == 1)
    def _():
        wbuf[pl.ds(0, 2), pl.ds(j, 1)] = hin[pl.ds(1, 2), :, own_cols].reshape(2, 1, hin.shape[1], 2 * HD)

    for yy in range(Y):
        theirs = pl.ds(pl.multiple_of((2 * yy + 1 - c) * HD, HD), HD)
        send(hout.at[:, theirs], wcat.at[mine_rows, pl.ds(yy * HD, HD)], wos, wor, twin)

    q_idx = compact_index(qtab[...])
    c_idx = compact_index(ctab[...])
    krows = q_idx.shape[0]

    @pl.when(handler)
    def _():
        mine = jnp.where(c == 0, q_idx, c_idx)
        row_id = iota((R, 128), 0).astype(F32)
        for k in range(krows):
            comp[:, k * 128:(k + 1) * 128] = onehot(row_id == mine[k:k + 1, :])

    rh = R // 2
    lower, upper = pl.ds(0, rh), pl.ds(rh, rh)

    @pl.when(handler)
    def _():
        drain(landed.at[pl.ds(0, S - 1)], s1r)
        xall[pl.ds(y, 1)] = dot(comp[...], landed[...].reshape(S * slots, FB)).astype(BF).reshape(1, R, FB)
        for d in range(1, X):
            send(xall.at[y, lower], xall.at[y, lower], xs.at[0], xr.at[0], (s, lax.rem(x + d, X)))
        for d in range(1, Y):
            send(xall.at[y, upper], xall.at[y, upper], xs.at[1], xr.at[1], (seq_of(z, lax.rem(y + d, Y), c), x))

    cidx[...] = q_idx
    half = krows // 2
    col_id = iota((128, R), 1).astype(F32)
    for k in range(half):
        column = as_column(cidx[pl.ds(half * c + k, 1), :])
        sel[k * 128:(k + 1) * 128, :] = onehot(column == col_id)

    @pl.when(jnp.logical_not(handler))
    def _():
        drain(xall.at[0, lower], xr.at[0])

    for d in range(1, Y):
        send(xall.at[y, lower], xall.at[y, lower], xs.at[2], xr.at[2], (seq_of(z, lax.rem(y + d, Y), c), x))

    @pl.when(jnp.logical_not(handler))
    def _():
        drain(xall.at[pl.ds(0, NY), lower], xr.at[1])

    if NY > 1:
        @pl.when(handler)
        def _():
            drain(xall.at[pl.ds(0, NY - 1), lower], xr.at[1])

    for d in range(1, X):
        for i in range(NY):
            u = i * X + x
            send(xall.at[u, upper], xall.at[u, upper], xs.at[3], xr.at[3], (s, lax.rem(x + d, X)))

    if X > 1:
        send(tok, tall.at[x], tks.at[0], tkr.at[0], (s, right))
    if X > 2:
        send(tok, tall.at[x], tks.at[1], tkr.at[1], (s, left))

    @pl.when(c == 0)
    def _():
        drain(wbuf.at[pl.ds(0, 1), pl.ds(0, nb - 1)], wsr)

    @pl.when(c == 1)
    def _():
        drain(wbuf.at[pl.ds(0, 2), pl.ds(0, nb - 1)], wsr)

    if Y > 1:
        drain(xall.at[pl.ds(0, Y - 1), lower], xr.at[2])
    if X > 1:
        drain(xall.at[pl.ds(0, NY * (X - 1)), upper], xr.at[3])

    def projected(i):
        total = None
        for yy in range(Y):
            term = dot(xall[yy], wbuf[i, 2 * yy:2 * yy + 2].reshape(FB, 2 * HD))
            total = term if total is None else total + term
        part[:, i] = total.astype(BF).reshape(Z, rz, 2 * HD)

    projected(0)

    @pl.when(c == 1)
    def _():
        projected(1)

    def sum_out(i, _):
        zt = lax.rem(z + 1 + i, Z)

        @pl.when(c == 0)
        def _():
            send(part.at[zt, pl.ds(0, 1)], rsum.at[z, pl.ds(0, 1)], rs, rr, (seq_of(zt, y, c), x))

        @pl.when(c == 1)
        def _():
            send(part.at[zt], rsum.at[z], rs, rr, (seq_of(zt, y, c), x))

        return 0

    lax.fori_loop(0, Z - 1, sum_out, 0)
    rsum[pl.ds(z, 1), 0:1] = part[pl.ds(z, 1), 0:1]

    @pl.when(c == 1)
    def _():
        rsum[pl.ds(z, 1), 1:2] = part[pl.ds(z, 1), 1:2]

    load_in.wait()

    def project_light(source, at, first):
        def one(i, _):
            term = dot(source[...], lw[i, pl.ds(pl.multiple_of(at * FX, FX), FX), :])
            if first:
                lmap[i] = term
            else:
                lmap[i] += term
            return 0

        lax.fori_loop(0, 3, one, 0)

    project_light(tok, x, True)

    th = T // 2
    front, back = pl.ds(0, th), pl.ds(th, th)
    if X > 1:
        drain(tall.at[0], tkr.at[0])
    if X > 2:
        send(tall.at[left, front], tall.at[left, front], tks.at[2], tkr.at[2], (s, right))
        drain(tall.at[0], tkr.at[1])
        send(tall.at[right, back], tall.at[right, back], tks.at[3], tkr.at[3], (s, left))

    @pl.when(c == 0)
    def _():
        drain(rsum.at[pl.ds(0, Z - 1), pl.ds(0, 1)], rr)
        rows = jnp.sum(rsum[:, 0].astype(F32), axis=0).astype(BF)
        qbuf[0] = rows[:, :HD]
        qbuf[1] = rows[:, HD:]
        send(qbuf.at[1], qbuf.at[0], qs, qr, twin)

    @pl.when(c == 1)
    def _():
        drain(rsum.at[pl.ds(0, Z - 1)], rr)
        for i in range(2):
            rows = jnp.sum(rsum[:, i].astype(F32), axis=0).astype(BF)
            for g in range(2):
                kv[g, i, pl.ds(z, 1)] = rows[:, g * HD:(g + 1) * HD].reshape(1, rz, HD)

        def kv_zero(i, _):
            zt = lax.rem(z + i, Z)
            send(kv.at[0, :, z], kv.at[1, :, z], kvs, kvr, (seq_of(zt, y, 0), x))
            return 0

        def kv_one(i, _):
            zt = lax.rem(z + 1 + i, Z)
            send(kv.at[1, :, z], kv.at[1, :, z], kvs, kvr, (seq_of(zt, y, 1), x))
            return 0

        lax.fori_loop(0, Z, kv_zero, 0)
        lax.fori_loop(0, Z - 1, kv_one, 0)

    if X > 1:
        project_light(tall.at[left], left, False)
    if X > 2:
        project_light(tall.at[right], right, False)
        drain(tall.at[0, front], tkr.at[2])
        drain(tall.at[0, back], tkr.at[3])
        project_light(tall.at[far], far, False)

    for g in range(2):
        for blk in range(T // LB):
            rows = slice(blk * LB, (blk + 1) * LB)
            cols = slice(g * HD, (g + 1) * HD)
            lheads[rows, cols] = softmax_value(
                lmap[0, rows, cols].astype(BF), lmap[1, rows, cols].astype(BF), lmap[2, rows, cols].astype(BF)
            )
    load_out.wait()

    def light_out(xt):
        return dot(lheads[...], lo[:, pl.ds(pl.multiple_of(xt * FX, FX), FX)])

    if X > 2:
        lsend[2] = light_out(far).astype(BF)
        send(lsend.at[2, front], lfar.at[0], lrs, lfr.at[0], (s, right))
        send(lsend.at[2, back], lfar.at[1], lrs, lfr.at[1], (s, left))
    if X > 1:
        lsend[0] = light_out(right).astype(BF)
    if X > 2:
        send(lsend.at[0, back], lrecv.at[0, back], lrs, lrr, (s, right))
        lsend[1] = light_out(left).astype(BF)
        send(lsend.at[1, front], lrecv.at[1, front], lrs, lrr, (s, left))
    elif X > 1:
        send(lsend.at[0], lrecv.at[0], lrs, lrr, (s, right))

    @pl.when(c == 0)
    def _():
        drain(kv.at[1], kvr)

    @pl.when(c == 1)
    def _():
        drain(qbuf.at[0], qr)
        drain(kv.at[1, :, pl.ds(0, Z - 1)], kvr)

    heads = softmax_value(qbuf[0], kv[1, 0].reshape(R, HD), kv[1, 1].reshape(R, HD))
    oz[pl.ds(z, 1)] = heads.reshape(1, rz, HD)

    def heads_out(i, _):
        zt = lax.rem(z + 1 + i, Z)
        send(oz.at[z], oz.at[z], ozs, ozr, (seq_of(zt, y, c), x))
        return 0

    lax.fori_loop(0, Z - 1, heads_out, 0)
    lacc[...] = light_out(x)

    if X > 2:
        drain(lfar.at[0], lfr.at[0])
        lsend[0, :th] = (lsend[0, :th].astype(F32) + lfar[0].astype(F32)).astype(BF)
        send(lsend.at[0, front], lrecv.at[0, front], lrs, lrr, (s, right))
        drain(lfar.at[1], lfr.at[1])
        lsend[1, th:] = (lsend[1, th:].astype(F32) + lfar[1].astype(F32)).astype(BF)
        send(lsend.at[1, back], lrecv.at[1, back], lrs, lrr, (s, left))

    drain(oz.at[pl.ds(0, Z - 1)], ozr)
    for d in range(1, Y):
        send(oz, oy.at[y], oys, oyr, (seq_of(z, lax.rem(y + d, Y), c), x))
    oy[pl.ds(y, 1)] = oz[...].reshape(1, Z, rz, HD)
    drain(wcat.at[pl.ds(0, FB // 2)], wor)
    if Y > 1:
        drain(oy.at[pl.ds(0, Y - 1)], oyr)
    total = None
    for yy in range(Y):
        term = dot_nt(oy[yy].reshape(R, HD), wcat[:, yy * HD:(yy + 1) * HD])
        total = term if total is None else total + term
    rmine[...] = total.astype(BF)
    send(rmine, rother, cs, cr, twin)
    drain(rother, cr)
    both = (total + rother[...].astype(F32)).astype(BF)
    rsel[...] = dot(sel[...], both).astype(BF).reshape(S // 2, slots, FB)

    block = pl.ds(pl.multiple_of(((z % 2) * Y + y) * FB, FB), FB)
    xq = z // 2

    def give(i, _):
        n = lax.rem(i + s + x * Y, S // 2)
        st = (S // 2) * c + n
        here = jnp.logical_and(st == s, xq == x)

        @pl.when(jnp.logical_not(here))
        def _():
            send(rsel.at[n], ret.at[x, :, block], rts, rtr, (st, xq))

        return 0

    lax.fori_loop(0, S // 2, give, 0)
    keeps = jnp.logical_and(xq == x, s // (S // 2) == c)

    @pl.when(keeps)
    def _():
        ret[pl.ds(x, 1), :, block] = rsel[pl.ds(lax.rem(s, S // 2), 1)]

    if X > 2:
        drain(lrecv, lrr)
        lacc[...] = lacc[...] + lrecv[0].astype(F32) + lrecv[1].astype(F32)
    elif X > 1:
        drain(lrecv.at[0], lrr)
        lacc[...] = lacc[...] + lrecv[0].astype(F32)
    onto = onehot(as_row(own_q) == iota((T, slots), 0).astype(F32))
    gates = as_column(gate[...])

    @pl.when(keeps)
    def _():
        drain(landed.at[pl.ds(0, nb * X - 1)], rtr)

    @pl.when(jnp.logical_not(keeps))
    def _():
        drain(landed.at[pl.ds(0, nb * X)], rtr)

    update = jnp.sum(ret[...].astype(F32), axis=0) * gates
    high = update.astype(BF)
    low = (update - high.astype(F32)).astype(BF)
    out[...] = (lacc[...] + dot(onto, high) + dot(onto, low)).astype(BF)

    if X > 1:
        drain(planes.at[:, pl.ds(0, X - 1)], s0s)
        drain(xall.at[pl.ds(0, NY * (X - 1)), upper], xs.at[3])
        drain(tall.at[0], tks.at[0])

    @pl.when(handler)
    def _():
        drain(landed.at[pl.ds(0, fan - 1)], s1s)
        if X > 1:
            drain(xall.at[pl.ds(0, X - 1), lower], xs.at[0])
        if Y > 1:
            drain(xall.at[pl.ds(0, Y - 1), upper], xs.at[1])

    @pl.when(jnp.logical_not(handler))
    def _():
        drain(landed.at[pl.ds(0, fan)], s1s)

    @pl.when(c == 0)
    def _():
        if Y > 1:
            drain(wbuf.at[pl.ds(0, 1), pl.ds(0, Y - 1)], wss)
        drain(wbuf.at[pl.ds(0, 2), pl.ds(0, Y)], wss)

    @pl.when(c == 1)
    def _():
        drain(wbuf.at[pl.ds(0, 1), pl.ds(0, Y)], wss)
        if Y > 1:
            drain(wbuf.at[pl.ds(0, 2), pl.ds(0, Y - 1)], wss)

    drain(wcat.at[pl.ds(0, FB // 2)], wos)
    if X > 2:
        drain(tall.at[0], tks.at[1])
        drain(tall.at[0, front], tks.at[2])
        drain(tall.at[0, back], tks.at[3])
        drain(lsend, lrs)
    elif X > 1:
        drain(lsend.at[0], lrs)
    if Y > 1:
        drain(xall.at[pl.ds(0, Y - 1), lower], xs.at[2])
        drain(oy.at[pl.ds(0, Y - 1)], oys)

    @pl.when(c == 0)
    def _():
        drain(rsum.at[pl.ds(0, Z - 1), pl.ds(0, 1)], rs)
        drain(qbuf.at[0], qs)

    @pl.when(c == 1)
    def _():
        drain(rsum.at[pl.ds(0, Z - 1)], rs)
        drain(kv.at[0], kvs)
        drain(kv.at[0, :, pl.ds(0, Z - 1)], kvs)

    drain(oz.at[pl.ds(0, Z - 1)], ozs)
    drain(rmine, cs)

    @pl.when(keeps)
    def _():
        drain(rsel.at[pl.ds(0, S // 2 - 1)], rts)

    @pl.when(jnp.logical_not(keeps))
    def _():
        drain(rsel, rts)


def body(dims, tokens, light_input, light_output, heavy_input, heavy_output, query_tokens, context_tokens, query_gate):
    Z, Y, X = dims
    S = Z * Y * 2
    nb = 2 * Y
    slots = query_tokens.shape[1]
    T, FX = tokens.shape
    R = S * T // 32
    rz = R // Z
    D = light_input.shape[1]
    LX = light_input.shape[2]
    hbm = pl.BlockSpec(memory_space=pl.ANY)
    dma = pltpu.SemaphoreType.DMA
    scratch = [
        pltpu.VMEM((T, FX), BF),
        pltpu.VMEM(heavy_input.shape, BF),
        pltpu.VMEM((FB // 2, 2 * Y * HD), BF),
        pltpu.VMEM((slots, S), jnp.int32),
        pltpu.VMEM((slots, S), jnp.int32),
        pltpu.VMEM((1, slots), F32),
        pltpu.VMEM((Y, 2, 2, slots, FB), BF),
        pltpu.VMEM((Y // X, X, 2, 2, slots, FB), BF),
        pltpu.VMEM((S, slots, FB), BF),
        pltpu.VMEM((R, S * slots), BF),
        pltpu.VMEM((S * slots // 2, R), BF),
        pltpu.VMEM((Y, R, FB), BF),
        pltpu.VMEM((2, nb, FB // 2, 2 * HD), BF),
        pltpu.VMEM((Z, 2, rz, 2 * HD), BF),
        pltpu.VMEM((Z, 2, rz, 2 * HD), BF),
        pltpu.VMEM((2, 2, Z, rz, HD), BF),
        pltpu.VMEM((2, rz, HD), BF),
        pltpu.VMEM((Z, rz, HD), BF),
        pltpu.VMEM((Y, Z, rz, HD), BF),
        pltpu.VMEM((FB, Y * HD), BF),
        pltpu.VMEM((R, FB), BF),
        pltpu.VMEM((R, FB), BF),
        pltpu.VMEM((S // 2, slots, FB), BF),
        pltpu.VMEM((X, slots, FX), BF),
        pltpu.VMEM((X, T, FX), BF),
        pltpu.VMEM((3, D, LX), BF),
        pltpu.VMEM((LX, D), BF),
        pltpu.VMEM((3, T, LX), F32),
        pltpu.VMEM((T, LX), BF),
        pltpu.VMEM((3, T, FX), BF),
        pltpu.VMEM((2, T // 2, FX), BF),
        pltpu.VMEM((2, T, FX), BF),
        pltpu.VMEM((T, FX), F32),
        pltpu.VMEM((S * slots // 128, 128), F32),
        *[dma(()) for _ in range(26)],
        dma((4,)), dma((4,)), dma((4,)), dma((4,)), dma((2,)), dma((6,)),
    ]
    return pl.pallas_call(
        functools.partial(kernel, dims),
        out_shape=jax.ShapeDtypeStruct((T, FX), BF),
        in_specs=[hbm] * 8,
        out_specs=pl.BlockSpec(memory_space=pltpu.VMEM),
        scratch_shapes=scratch,
        compiler_params=pltpu.CompilerParams(collective_id=0, has_side_effects=True, vmem_limit_bytes=56 << 20),
    )(
        tokens, light_input, light_output, heavy_input, heavy_output.T, query_tokens.T, context_tokens.T, query_gate
    )


def solution(mesh):
    X = mesh.shape["head"]
    Z = 2 * X
    dims = (Z, mesh.shape["seq"] // (2 * Z), X)
    placed = (
        P("seq", "head"),
        P(None, None, "head"),
        P("head", None),
        P(None, "seq", "head"),
        P("head", "seq"),
        P(),
        P(),
        P("seq", None),
    )
    return jax.shard_map(
        functools.partial(body, dims), mesh=mesh, in_specs=placed, out_specs=P("seq", "head"), check_vma=False
    )
```

```python
import functools
import math

import jax
import jax.numpy as jnp
from jax import lax
from jax.experimental import pallas as pl
from jax.experimental.pallas import tpu as pltpu
from jax.sharding import PartitionSpec as P

HD = 128
LB = 128
FB = 128
BF = jnp.bfloat16
F32 = jnp.float32


def dot(a, b):
    return jnp.dot(a, b, preferred_element_type=F32)


def dot_nt(a, b):
    return lax.dot_general(a, b, (((1,), (1,)), ((), ())), preferred_element_type=F32)


def iota(shape, dim):
    return lax.broadcasted_iota(jnp.int32, shape, dim)


def as_column(row):
    n = row.shape[1]
    wide = jnp.broadcast_to(row, (n, n))
    return jnp.sum(jnp.where(iota((n, n), 0) == iota((n, n), 1), wide, 0.0), axis=1, keepdims=True)


def as_row(column):
    n = column.shape[0]
    wide = jnp.broadcast_to(column, (n, n))
    return jnp.sum(jnp.where(iota((n, n), 0) == iota((n, n), 1), wide, 0.0), axis=0, keepdims=True)


def onehot(hit):
    return jnp.where(hit, 1.0, 0.0).astype(BF)


def compact_index(table):
    slots, shards = table.shape
    per = 128 // slots
    rows = shards // per
    spread = onehot(iota((128, slots), 0) % slots == iota((128, slots), 1))
    tiled = dot(spread, table.astype(F32).astype(BF))
    keep = iota((128, shards), 1) % per == iota((128, shards), 0) // slots
    join = onehot(iota((rows, shards), 1) // per == iota((rows, shards), 0))
    flat = dot_nt(join, jnp.where(keep, tiled, 0.0).astype(BF))
    live = flat >= 0.0
    marks = onehot(live)
    before = dot(marks, onehot(iota((128, 128), 0) < iota((128, 128), 1)))
    in_row = dot(marks, jnp.ones((128, 128), BF))
    above = dot(onehot(iota((rows, rows), 1) < iota((rows, rows), 0)), in_row.astype(BF))
    return jnp.where(live, before + above, -1.0)


def softmax_value(q, k, v):
    scores = dot_nt(q, k) * (1.0 / math.sqrt(HD))
    expanded = jnp.exp(scores - jnp.max(scores, axis=-1, keepdims=True))
    totals = jnp.sum(expanded, axis=-1, keepdims=True)
    return (dot(expanded.astype(BF), v) / totals).astype(BF)


def kernel(
    dims,
    tok_any, lin, lout, hin_any, hout_any, qtab_any, ctab_any, gate_any,
    out,
    tok, hin, hout, qtab, ctab, gate,
    picks, planes, landed, comp, sel, xall, wbuf, part, rsum, kv, qbuf, oz, oy,
    wcat, rmine, rother, rsel, ret,
    tall, lw, lo, lmap, lheads, lsend, lfar, lrecv, lacc, cidx,
    s0s, s0r, s1s, s1r, wss, wsr, wos, wor, rs, rr, kvs, kvr, qs, qr,
    ozs, ozr, oys, oyr, cs, cr, rts, rtr, lrs, lrr, lis, los,
    tks, tkr, xs, xr, lfr, ins,
):
    Z, Y, X = dims
    NY = Y // X
    nb = 2 * Y
    S = Z * Y * 2
    R = comp.shape[0]
    rz = R // Z
    slots = qtab.shape[0]
    T = tok.shape[0]
    FX = tok.shape[1]
    s = lax.axis_index("seq")
    x = lax.axis_index("head")
    z = s // (2 * Y)
    y = (s // 2) % Y
    c = s % 2
    right, left = lax.rem(x + 1, X), lax.rem(x + X - 1, X)
    far = lax.rem(x + 2, X)

    def seq_of(zz, yy, cc):
        return (zz * Y + yy) * 2 + cc

    twin = (seq_of(z, y, 1 - c), x)
    others = sorted(range(1, Z), key=lambda d: -min(d, Z - d))

    def send(src, dst, ss, rsem, to):
        pltpu.make_async_remote_copy(
            src_ref=src, dst_ref=dst, send_sem=ss, recv_sem=rsem,
            device_id=to, device_id_type=pl.DeviceIdType.MESH,
        ).start()

    def drain(ref, sem):
        pltpu.make_async_copy(ref, ref, sem).wait()

    barrier = pltpu.get_barrier_semaphore()

    def greet(to):
        pl.semaphore_signal(barrier, inc=1, device_id=to, device_id_type=pl.DeviceIdType.MESH)

    unit = (y + c * (Y // 2)) % Y
    handler = unit % X == x

    for d in range(1, nb):
        jt = lax.rem(2 * y + c + d, nb)
        greet((seq_of(z, jt // 2, jt % 2), x))
    for d in range(1, X):
        greet((s, lax.rem(x + d, X)))

    @pl.when(handler)
    def _():
        def greet_plane(i, _):
            greet((lax.rem(s + 1 + i, S), x))
            return 0

        lax.fori_loop(0, S - 1, greet_plane, 0)

    fetches = [
        pltpu.make_async_copy(src, dst, ins.at[i])
        for i, (src, dst) in enumerate((
            (qtab_any, qtab), (ctab_any, ctab), (tok_any, tok), (hin_any, hin), (hout_any, hout), (gate_any, gate),
        ))
    ]
    for fetch in fetches:
        fetch.start()
    load_in = pltpu.make_async_copy(lin, lw, lis)
    load_out = pltpu.make_async_copy(lout, lo, los)
    load_in.start()
    load_out.start()

    fetches[0].wait()
    fetches[1].wait()
    here_s = iota((slots, S), 1) == s
    own_q = jnp.sum(jnp.where(here_s, qtab[...].astype(F32), 0.0), axis=1, keepdims=True)
    own_c = jnp.sum(jnp.where(here_s, ctab[...].astype(F32), 0.0), axis=1, keepdims=True)
    fetches[2].wait()
    for i, column in enumerate((own_q, own_c)):
        want = onehot(column == iota((slots, T), 1).astype(F32))
        rows = dot(want, tok[...]).astype(BF)
        for b in range(nb):
            picks[b % Y, b // Y, i] = rows[:, b * FB:(b + 1) * FB]

    met = (nb - 1) + (X - 1) + NY * Z * 2

    @pl.when(handler)
    def _():
        pl.semaphore_wait(barrier, met - 1)

    @pl.when(jnp.logical_not(handler))
    def _():
        pl.semaphore_wait(barrier, met)

    for d in range(1, X):
        xt = lax.rem(x + d, X)
        for i in range(NY):
            send(picks.at[i * X + xt], planes.at[i, x], s0s, s0r, (s, xt))
    for i in range(NY):
        planes[i, pl.ds(x, 1)] = picks[pl.ds(i * X + x, 1)]

    mine_rows = pl.ds(pl.multiple_of(c * (FB // 2), FB // 2), FB // 2)
    fetches[3].wait()
    fetches[4].wait()
    fetches[5].wait()
    for yy in range(Y):
        wcat[mine_rows, yy * HD:(yy + 1) * HD] = hout[:, pl.ds(pl.multiple_of((2 * yy + c) * HD, HD), HD)]
    if X > 1:
        drain(planes.at[:, pl.ds(0, X - 1)], s0r)

    fan = NY * Z * 2

    def route(i, _):
        n = lax.rem(i + 2 * z + c, fan)
        yi = n // (2 * Z)
        zt = (n // 2) % Z
        ct = n % 2
        st = seq_of(zt, (yi * X + x + Y - ct * (Y // 2)) % Y, ct)

        @pl.when(st != s)
        def _():
            send(planes.at[yi, zt // 2, zt % 2, ct], landed.at[s], s1s, s1r, (st, x))

        return 0

    lax.fori_loop(0, fan, route, 0)

    @pl.when(handler)
    def _():
        landed[pl.ds(s, 1)] = planes[
            pl.ds(unit // X, 1), pl.ds(z // 2, 1), pl.ds(z % 2, 1), pl.ds(c, 1)
        ].reshape(1, slots, FB)

    th = T // 2
    front, back = pl.ds(0, th), pl.ds(th, th)
    if X > 2:
        send(tok.at[front], tall.at[x, front], tks.at[0], tkr.at[0], (s, right))
        send(tok.at[back], tall.at[x, back], tks.at[1], tkr.at[1], (s, left))
    elif X > 1:
        send(tok, tall.at[x], tks.at[0], tkr.at[0], (s, right))

    j = 2 * y + c

    def weights_out(i, _):
        jt = lax.rem(j + 1 + i, nb)
        yt = jt // 2
        ct = jt % 2
        cols = pl.ds(pl.multiple_of(yt * 2 * HD, 2 * HD), 2 * HD)

        @pl.when(ct == 0)
        def _():
            send(hin.at[pl.ds(0, 1), :, cols], wbuf.at[pl.ds(0, 1), j], wss, wsr, (seq_of(z, yt, ct), x))

        @pl.when(ct == 1)
        def _():
            send(hin.at[pl.ds(1, 2), :, cols], wbuf.at[pl.ds(0, 2), j], wss, wsr, (seq_of(z, yt, ct), x))

        return 0

    lax.fori_loop(0, nb - 1, weights_out, 0)
    own_cols = pl.ds(pl.multiple_of(y * 2 * HD, 2 * HD), 2 * HD)

    @pl.when(c == 0)
    def _():
        wbuf[pl.ds(0, 1), pl.ds(j, 1)] = hin[pl.ds(0, 1), :, own_cols].reshape(1, 1, hin.shape[1], 2 * HD)

    @pl.when(c == 1)
    def _():
        wbuf[pl.ds(0, 2), pl.ds(j, 1)] = hin[pl.ds(1, 2), :, own_cols].reshape(2, 1, hin.shape[1], 2 * HD)

    for yy in range(Y):
        theirs = pl.ds(pl.multiple_of((2 * yy + 1 - c) * HD, HD), HD)
        send(hout.at[:, theirs], wcat.at[mine_rows, pl.ds(yy * HD, HD)], wos, wor, twin)

    q_idx = compact_index(qtab[...])
    c_idx = compact_index(ctab[...])
    krows = q_idx.shape[0]

    @pl.when(handler)
    def _():
        mine = jnp.where(c == 0, q_idx, c_idx)
        row_id = iota((R, 128), 0).astype(F32)
        for k in range(krows):
            comp[:, k * 128:(k + 1) * 128] = onehot(row_id == mine[k:k + 1, :])

    rh = R // 2
    lower, upper = pl.ds(0, rh), pl.ds(rh, rh)

    @pl.when(handler)
    def _():
        drain(landed.at[pl.ds(0, S - 1)], s1r)
        for part_rows in (lower, upper):
            xall[pl.ds(unit, 1), part_rows] = dot(
                comp[part_rows, :], landed[...].reshape(S * slots, FB)
            ).astype(BF).reshape(1, rh, FB)
            if part_rows is lower:
                for d in range(1, X):
                    send(xall.at[unit, lower], xall.at[unit, lower], xs.at[0], xr.at[0], (s, lax.rem(x + d, X)))
            else:
                for d in range(1, Y):
                    send(
                        xall.at[unit, upper], xall.at[unit, upper], xs.at[1], xr.at[1],
                        (seq_of(z, lax.rem(y + d, Y), c), x),
                    )

    cidx[...] = q_idx
    half = krows // 2
    per_z = krows // Z

    def back_row(k):
        ahead = jnp.where(c == 0, Z // 2 - 1 - k // per_z, Z // 2 + k // per_z)
        return lax.rem(z + ahead, Z) * per_z + lax.rem(k + y, per_z)

    col_id = iota((128, R), 1).astype(F32)
    for k in range(half):
        column = as_column(cidx[pl.ds(back_row(k), 1), :])
        sel[k * 128:(k + 1) * 128, :] = onehot(column == col_id)

    @pl.when(jnp.logical_not(handler))
    def _():
        drain(xall.at[0, lower], xr.at[0])

    for d in range(1, Y):
        send(xall.at[unit, lower], xall.at[unit, lower], xs.at[2], xr.at[2], (seq_of(z, lax.rem(y + d, Y), c), x))

    @pl.when(jnp.logical_not(handler))
    def _():
        drain(xall.at[pl.ds(0, NY), lower], xr.at[1])

    if NY > 1:
        @pl.when(handler)
        def _():
            drain(xall.at[pl.ds(0, NY - 1), lower], xr.at[1])

    for d in range(1, X):
        for i in range(NY):
            u = i * X + x
            send(xall.at[u, upper], xall.at[u, upper], xs.at[3], xr.at[3], (s, lax.rem(x + d, X)))

    if X > 2:
        drain(tall.at[0, front], tkr.at[0])
        send(tall.at[left, front], tall.at[left, front], tks.at[2], tkr.at[2], (s, right))
        drain(tall.at[0, back], tkr.at[1])
        send(tall.at[right, back], tall.at[right, back], tks.at[3], tkr.at[3], (s, left))
        send(tok.at[back], tall.at[x, back], tks.at[4], tkr.at[4], (s, right))
        send(tok.at[front], tall.at[x, front], tks.at[5], tkr.at[5], (s, left))
    elif X > 1:
        drain(tall.at[0], tkr.at[0])

    @pl.when(c == 0)
    def _():
        drain(wbuf.at[pl.ds(0, 1), pl.ds(0, nb - 1)], wsr)

    @pl.when(c == 1)
    def _():
        drain(wbuf.at[pl.ds(0, 2), pl.ds(0, nb - 1)], wsr)

    if Y > 1:
        drain(xall.at[pl.ds(0, Y - 1), lower], xr.at[2])
    if X > 1:
        drain(xall.at[pl.ds(0, NY * (X - 1)), upper], xr.at[3])

    def projected(i):
        total = None
        for yy in range(Y):
            term = dot(xall[yy], wbuf[i, 2 * yy:2 * yy + 2].reshape(FB, 2 * HD))
            total = term if total is None else total + term
        part[:, i] = total.astype(BF).reshape(Z, rz, 2 * HD)

    projected(0)

    @pl.when(c == 0)
    def _():
        for d in others:
            zt = lax.rem(z + d, Z)
            send(part.at[zt, pl.ds(0, 1)], rsum.at[z, pl.ds(0, 1)], rs, rr, (seq_of(zt, y, c), x))

    @pl.when(c == 1)
    def _():
        projected(1)
        for d in others:
            zt = lax.rem(z + d, Z)
            send(part.at[zt], rsum.at[z], rs, rr, (seq_of(zt, y, c), x))

    rsum[pl.ds(z, 1), 0:1] = part[pl.ds(z, 1), 0:1]

    @pl.when(c == 1)
    def _():
        rsum[pl.ds(z, 1), 1:2] = part[pl.ds(z, 1), 1:2]

    load_in.wait()

    def project_light(source, at, first):
        def one(i, _):
            term = dot(source[...], lw[i, pl.ds(pl.multiple_of(at * FX, FX), FX), :])
            if first:
                lmap[i] = term
            else:
                lmap[i] += term
            return 0

        lax.fori_loop(0, 3, one, 0)

    project_light(tok, x, True)

    @pl.when(c == 0)
    def _():
        drain(rsum.at[pl.ds(0, Z - 1), pl.ds(0, 1)], rr)
        rows = jnp.sum(rsum[:, 0].astype(F32), axis=0).astype(BF)
        qbuf[0] = rows[:, :HD]
        qbuf[1] = rows[:, HD:]
        send(qbuf.at[1], qbuf.at[0], qs, qr, twin)

    @pl.when(c == 1)
    def _():
        drain(rsum.at[pl.ds(0, Z - 1)], rr)
        for i in range(2):
            rows = jnp.sum(rsum[:, i].astype(F32), axis=0).astype(BF)
            for g in range(2):
                kv[g, i, pl.ds(z, 1)] = rows[:, g * HD:(g + 1) * HD].reshape(1, rz, HD)

        for d in [*others, 0]:
            zt = lax.rem(z + d, Z)
            send(kv.at[0, :, z], kv.at[1, :, z], kvs, kvr, (seq_of(zt, y, 0), x))
            if d:
                send(kv.at[1, :, z], kv.at[1, :, z], kvs, kvr, (seq_of(zt, y, 1), x))

    if X > 2:
        drain(tall.at[0, front], tkr.at[2])
        drain(tall.at[0, back], tkr.at[3])
        drain(tall.at[0, back], tkr.at[4])
        drain(tall.at[0, front], tkr.at[5])
    if X > 1:
        project_light(tall.at[left], left, False)
    if X > 2:
        project_light(tall.at[right], right, False)
        project_light(tall.at[far], far, False)

    for g in range(2):
        for blk in range(T // LB):
            rows = slice(blk * LB, (blk + 1) * LB)
            cols = slice(g * HD, (g + 1) * HD)
            lheads[rows, cols] = softmax_value(
                lmap[0, rows, cols].astype(BF), lmap[1, rows, cols].astype(BF), lmap[2, rows, cols].astype(BF)
            )
    load_out.wait()

    def light_out(xt):
        return dot(lheads[...], lo[:, pl.ds(pl.multiple_of(xt * FX, FX), FX)])

    if X > 2:
        lsend[2] = light_out(far).astype(BF)
        send(lsend.at[2, front], lfar.at[0], lrs, lfr.at[0], (s, right))
        send(lsend.at[2, back], lfar.at[1], lrs, lfr.at[1], (s, left))
    if X > 1:
        lsend[0] = light_out(right).astype(BF)
    if X > 2:
        send(lsend.at[0, back], lrecv.at[0, back], lrs, lrr, (s, right))
        lsend[1] = light_out(left).astype(BF)
        send(lsend.at[1, front], lrecv.at[1, front], lrs, lrr, (s, left))
    elif X > 1:
        send(lsend.at[0], lrecv.at[0], lrs, lrr, (s, right))

    @pl.when(c == 0)
    def _():
        drain(kv.at[1], kvr)

    @pl.when(c == 1)
    def _():
        drain(qbuf.at[0], qr)
        drain(kv.at[1, :, pl.ds(0, Z - 1)], kvr)

    heads = softmax_value(qbuf[0], kv[1, 0].reshape(R, HD), kv[1, 1].reshape(R, HD))
    oz[pl.ds(z, 1)] = heads.reshape(1, rz, HD)

    for d in others:
        zt = lax.rem(z + d, Z)
        send(oz.at[z], oz.at[z], ozs, ozr, (seq_of(zt, y, c), x))

    lacc[...] = light_out(x)

    drain(oz.at[pl.ds(0, Z - 1)], ozr)
    for d in range(1, Y):
        send(oz, oy.at[y], oys, oyr, (seq_of(z, lax.rem(y + d, Y), c), x))
    oy[pl.ds(y, 1)] = oz[...].reshape(1, Z, rz, HD)
    if X > 2:
        drain(lfar.at[0], lfr.at[0])
        lsend[0, :th] = (lsend[0, :th].astype(F32) + lfar[0].astype(F32)).astype(BF)
        send(lsend.at[0, front], lrecv.at[0, front], lrs, lrr, (s, right))
        drain(lfar.at[1], lfr.at[1])
        lsend[1, th:] = (lsend[1, th:].astype(F32) + lfar[1].astype(F32)).astype(BF)
        send(lsend.at[1, back], lrecv.at[1, back], lrs, lrr, (s, left))

    drain(wcat.at[pl.ds(0, FB // 2)], wor)
    if Y > 1:
        drain(oy.at[pl.ds(0, Y - 1)], oyr)
    total = None
    for yy in range(Y):
        term = dot_nt(oy[yy].reshape(R, HD), wcat[:, yy * HD:(yy + 1) * HD])
        total = term if total is None else total + term
    rmine[...] = total.astype(BF)
    send(rmine, rother, cs, cr, twin)
    drain(rother, cr)
    drain(rmine, cs)
    both = (total + rother[...].astype(F32)).astype(BF)
    rmine[...] = both

    block = pl.ds(pl.multiple_of(((z % 2) * Y + y) * FB, FB), FB)
    xq = z // 2

    step = S // 2 // half

    def choose(k, _):
        chosen = dot(sel[pl.ds(pl.multiple_of(k * 128, 128), 128), :], rmine[...]).astype(BF)
        rsel[pl.ds(k * step, step)] = chosen.reshape(step, slots, FB)
        for i in range(step):
            st = back_row(k) * step + i
            here = jnp.logical_and(st == s, xq == x)

            @pl.when(jnp.logical_not(here))
            def _():
                send(rsel.at[k * step + i], ret.at[x, :, block], rts, rtr, (st, xq))

            @pl.when(here)
            def _():
                ret[pl.ds(x, 1), :, block] = rsel[pl.ds(k * step + i, 1)]

        return 0

    lax.fori_loop(0, half, choose, 0)
    keeps = jnp.logical_and(xq == x, c == 0)

    if X > 2:
        drain(lrecv, lrr)
        lacc[...] = lacc[...] + lrecv[0].astype(F32) + lrecv[1].astype(F32)
    elif X > 1:
        drain(lrecv.at[0], lrr)
        lacc[...] = lacc[...] + lrecv[0].astype(F32)
    onto = onehot(as_row(own_q) == iota((T, slots), 0).astype(F32))
    gates = as_column(gate[...])

    @pl.when(keeps)
    def _():
        drain(landed.at[pl.ds(0, nb * X - 1)], rtr)

    @pl.when(jnp.logical_not(keeps))
    def _():
        drain(landed.at[pl.ds(0, nb * X)], rtr)

    update = jnp.sum(ret[...].astype(F32), axis=0) * gates
    high = update.astype(BF)
    low = (update - high.astype(F32)).astype(BF)
    out[...] = (lacc[...] + dot(onto, high) + dot(onto, low)).astype(BF)

    if X > 1:
        drain(planes.at[:, pl.ds(0, X - 1)], s0s)
        drain(xall.at[pl.ds(0, NY * (X - 1)), upper], xs.at[3])
        drain(tall.at[0, front] if X > 2 else tall.at[0], tks.at[0])

    @pl.when(handler)
    def _():
        drain(landed.at[pl.ds(0, fan - 1)], s1s)
        if X > 1:
            drain(xall.at[pl.ds(0, X - 1), lower], xs.at[0])
        if Y > 1:
            drain(xall.at[pl.ds(0, Y - 1), upper], xs.at[1])

    @pl.when(jnp.logical_not(handler))
    def _():
        drain(landed.at[pl.ds(0, fan)], s1s)

    @pl.when(c == 0)
    def _():
        if Y > 1:
            drain(wbuf.at[pl.ds(0, 1), pl.ds(0, Y - 1)], wss)
        drain(wbuf.at[pl.ds(0, 2), pl.ds(0, Y)], wss)

    @pl.when(c == 1)
    def _():
        drain(wbuf.at[pl.ds(0, 1), pl.ds(0, Y)], wss)
        if Y > 1:
            drain(wbuf.at[pl.ds(0, 2), pl.ds(0, Y - 1)], wss)

    drain(wcat.at[pl.ds(0, FB // 2)], wos)
    if X > 2:
        drain(tall.at[0, back], tks.at[1])
        drain(tall.at[0, back], tks.at[4])
        drain(tall.at[0, front], tks.at[5])
        drain(tall.at[0, front], tks.at[2])
        drain(tall.at[0, back], tks.at[3])
        drain(lsend, lrs)
    elif X > 1:
        drain(lsend.at[0], lrs)
    if Y > 1:
        drain(xall.at[pl.ds(0, Y - 1), lower], xs.at[2])
        drain(oy.at[pl.ds(0, Y - 1)], oys)

    @pl.when(c == 0)
    def _():
        drain(rsum.at[pl.ds(0, Z - 1), pl.ds(0, 1)], rs)
        drain(qbuf.at[0], qs)

    @pl.when(c == 1)
    def _():
        drain(rsum.at[pl.ds(0, Z - 1)], rs)
        drain(kv.at[0], kvs)
        drain(kv.at[0, :, pl.ds(0, Z - 1)], kvs)

    drain(oz.at[pl.ds(0, Z - 1)], ozs)

    @pl.when(keeps)
    def _():
        drain(rsel.at[pl.ds(0, S // 2 - 1)], rts)

    @pl.when(jnp.logical_not(keeps))
    def _():
        drain(rsel, rts)


def body(dims, tokens, light_input, light_output, heavy_input, heavy_output, query_tokens, context_tokens, query_gate):
    Z, Y, X = dims
    S = Z * Y * 2
    nb = 2 * Y
    slots = query_tokens.shape[1]
    T, FX = tokens.shape
    R = S * T // 32
    rz = R // Z
    D = light_input.shape[1]
    LX = light_input.shape[2]
    hbm = pl.BlockSpec(memory_space=pl.ANY)
    dma = pltpu.SemaphoreType.DMA
    scratch = [
        pltpu.VMEM((T, FX), BF),
        pltpu.VMEM(heavy_input.shape, BF),
        pltpu.VMEM((FB // 2, 2 * Y * HD), BF),
        pltpu.VMEM((slots, S), jnp.int32),
        pltpu.VMEM((slots, S), jnp.int32),
        pltpu.VMEM((1, slots), F32),
        pltpu.VMEM((Y, 2, 2, slots, FB), BF),
        pltpu.VMEM((Y // X, X, 2, 2, slots, FB), BF),
        pltpu.VMEM((S, slots, FB), BF),
        pltpu.VMEM((R, S * slots), BF),
        pltpu.VMEM((S * slots // 2, R), BF),
        pltpu.VMEM((Y, R, FB), BF),
        pltpu.VMEM((2, nb, FB // 2, 2 * HD), BF),
        pltpu.VMEM((Z, 2, rz, 2 * HD), BF),
        pltpu.VMEM((Z, 2, rz, 2 * HD), BF),
        pltpu.VMEM((2, 2, Z, rz, HD), BF),
        pltpu.VMEM((2, rz, HD), BF),
        pltpu.VMEM((Z, rz, HD), BF),
        pltpu.VMEM((Y, Z, rz, HD), BF),
        pltpu.VMEM((FB, Y * HD), BF),
        pltpu.VMEM((R, FB), BF),
        pltpu.VMEM((R, FB), BF),
        pltpu.VMEM((S // 2, slots, FB), BF),
        pltpu.VMEM((X, slots, FX), BF),
        pltpu.VMEM((X, T, FX), BF),
        pltpu.VMEM((3, D, LX), BF),
        pltpu.VMEM((LX, D), BF),
        pltpu.VMEM((3, T, LX), F32),
        pltpu.VMEM((T, LX), BF),
        pltpu.VMEM((3, T, FX), BF),
        pltpu.VMEM((2, T // 2, FX), BF),
        pltpu.VMEM((2, T, FX), BF),
        pltpu.VMEM((T, FX), F32),
        pltpu.VMEM((S * slots // 128, 128), F32),
        *[dma(()) for _ in range(26)],
        dma((6,)), dma((6,)), dma((4,)), dma((4,)), dma((2,)), dma((6,)),
    ]
    return pl.pallas_call(
        functools.partial(kernel, dims),
        out_shape=jax.ShapeDtypeStruct((T, FX), BF),
        in_specs=[hbm] * 8,
        out_specs=pl.BlockSpec(memory_space=pltpu.VMEM),
        scratch_shapes=scratch,
        compiler_params=pltpu.CompilerParams(collective_id=0, has_side_effects=True, vmem_limit_bytes=48 << 20),
    )(*(
        pltpu.with_memory_space_constraint(a, pltpu.HBM)
        for a in (
            tokens, light_input, light_output, heavy_input, heavy_output.T, query_tokens.T, context_tokens.T, query_gate
        )
    ))


def solution(mesh):
    X = mesh.shape["head"]
    Z = 2 * X
    dims = (Z, mesh.shape["seq"] // (2 * Z), X)
    placed = (
        P("seq", "head"),
        P(None, None, "head"),
        P("head", None),
        P(None, "seq", "head"),
        P("head", "seq"),
        P(),
        P(),
        P("seq", None),
    )
    return jax.shard_map(
        functools.partial(body, dims), mesh=mesh, in_specs=placed, out_specs=P("seq", "head"), check_vma=False
    )
```

```python
import functools
import math

import jax
import jax.numpy as jnp
from jax import lax
from jax.experimental import pallas as pl
from jax.experimental.pallas import tpu as pltpu
from jax.sharding import PartitionSpec as P

HD = 128
LB = 128
FB = 128
BF = jnp.bfloat16
F32 = jnp.float32


def dot(a, b):
    return jnp.dot(a, b, preferred_element_type=F32)


def dot_nt(a, b):
    return lax.dot_general(a, b, (((1,), (1,)), ((), ())), preferred_element_type=F32)


def iota(shape, dim):
    return lax.broadcasted_iota(jnp.int32, shape, dim)


def as_column(row):
    n = row.shape[1]
    wide = jnp.broadcast_to(row, (n, n))
    return jnp.sum(jnp.where(iota((n, n), 0) == iota((n, n), 1), wide, 0.0), axis=1, keepdims=True)


def as_row(column):
    n = column.shape[0]
    wide = jnp.broadcast_to(column, (n, n))
    return jnp.sum(jnp.where(iota((n, n), 0) == iota((n, n), 1), wide, 0.0), axis=0, keepdims=True)


def onehot(hit):
    return jnp.where(hit, 1.0, 0.0).astype(BF)


def compact_index(table):
    slots, shards = table.shape
    per = 128 // slots
    rows = shards // per
    spread = onehot(iota((128, slots), 0) % slots == iota((128, slots), 1))
    tiled = dot(spread, table.astype(F32).astype(BF))
    keep = iota((128, shards), 1) % per == iota((128, shards), 0) // slots
    join = onehot(iota((rows, shards), 1) // per == iota((rows, shards), 0))
    flat = dot_nt(join, jnp.where(keep, tiled, 0.0).astype(BF))
    live = flat >= 0.0
    marks = onehot(live)
    before = dot(marks, onehot(iota((128, 128), 0) < iota((128, 128), 1)))
    in_row = dot(marks, jnp.ones((128, 128), BF))
    above = dot(onehot(iota((rows, rows), 1) < iota((rows, rows), 0)), in_row.astype(BF))
    return jnp.where(live, before + above, -1.0)


def softmax_value(q, k, v):
    scores = dot_nt(q, k) * (1.0 / math.sqrt(HD))
    expanded = jnp.exp(scores - jnp.max(scores, axis=-1, keepdims=True))
    totals = jnp.sum(expanded, axis=-1, keepdims=True)
    return (dot(expanded.astype(BF), v) / totals).astype(BF)


def kernel(
    dims,
    tok_any, lin, lout, hin_any, hout_any, qtab_any, ctab_any, gate_any,
    out,
    tok, hin, hout, qtab, ctab, gate,
    picks, planes, landed, comp, sel, xall, wbuf, part, rsum, kv, qbuf, oy,
    wcat, rmine, rother, rsel, ret,
    tall, lw, lo, lmap, lheads, lsend, lfar, lrecv, lacc, cidx,
    s0s, s0r, s1s, s1r, wss, wsr, wos, wor, qs, qr,
    ozs, oys, oyr, cs, cr, rts, rtr, lrs, lrr, lis, los,
    tks, tkr, xs, xr, lfr, ins, rs, rr, kvs, kvr, ozr,
):
    Z, Y, X = dims
    NY = Y // X
    nb = 2 * Y
    S = Z * Y * 2
    R = comp.shape[0]
    rz = R // Z
    slots = qtab.shape[0]
    T = tok.shape[0]
    FX = tok.shape[1]
    s = lax.axis_index("seq")
    x = lax.axis_index("head")
    z = s // (2 * Y)
    y = (s // 2) % Y
    c = s % 2
    right, left = lax.rem(x + 1, X), lax.rem(x + X - 1, X)
    far = lax.rem(x + 2, X)

    def seq_of(zz, yy, cc):
        return (zz * Y + yy) * 2 + cc

    twin = (seq_of(z, y, 1 - c), x)
    others = sorted(range(1, Z), key=lambda d: -min(d, Z - d))

    def send(src, dst, ss, rsem, to):
        pltpu.make_async_remote_copy(
            src_ref=src, dst_ref=dst, send_sem=ss, recv_sem=rsem,
            device_id=to, device_id_type=pl.DeviceIdType.MESH,
        ).start()

    def drain(ref, sem):
        pltpu.make_async_copy(ref, ref, sem).wait()

    barrier = pltpu.get_barrier_semaphore()

    def greet(to):
        pl.semaphore_signal(barrier, inc=1, device_id=to, device_id_type=pl.DeviceIdType.MESH)

    unit = (y + c * (Y // 2)) % Y
    handler = unit % X == x

    for d in range(1, nb):
        jt = lax.rem(2 * y + c + d, nb)
        greet((seq_of(z, jt // 2, jt % 2), x))
    for d in range(1, X):
        greet((s, lax.rem(x + d, X)))

    @pl.when(handler)
    def _():
        def greet_plane(i, _):
            greet((lax.rem(s + 1 + i, S), x))
            return 0

        lax.fori_loop(0, S - 1, greet_plane, 0)

    fetches = [
        pltpu.make_async_copy(src, dst, ins.at[i])
        for i, (src, dst) in enumerate((
            (qtab_any, qtab), (ctab_any, ctab), (tok_any, tok), (hin_any, hin), (hout_any, hout), (gate_any, gate),
        ))
    ]
    for fetch in fetches:
        fetch.start()
    load_in = pltpu.make_async_copy(lin, lw, lis)
    load_out = pltpu.make_async_copy(lout, lo, los)
    load_in.start()
    load_out.start()

    fetches[0].wait()
    fetches[1].wait()
    here_s = iota((slots, S), 1) == s
    own_q = jnp.sum(jnp.where(here_s, qtab[...].astype(F32), 0.0), axis=1, keepdims=True)
    own_c = jnp.sum(jnp.where(here_s, ctab[...].astype(F32), 0.0), axis=1, keepdims=True)
    fetches[2].wait()
    for i, column in enumerate((own_q, own_c)):
        want = onehot(column == iota((slots, T), 1).astype(F32))
        rows = dot(want, tok[...]).astype(BF)
        for b in range(nb):
            picks[b % Y, b // Y, i] = rows[:, b * FB:(b + 1) * FB]

    met = (nb - 1) + (X - 1) + NY * Z * 2

    @pl.when(handler)
    def _():
        pl.semaphore_wait(barrier, met - 1)

    @pl.when(jnp.logical_not(handler))
    def _():
        pl.semaphore_wait(barrier, met)

    for d in range(1, X):
        xt = lax.rem(x + d, X)
        for i in range(NY):
            send(picks.at[i * X + xt], planes.at[i, x], s0s, s0r, (s, xt))
    for i in range(NY):
        planes[i, pl.ds(x, 1)] = picks[pl.ds(i * X + x, 1)]

    mine_rows = pl.ds(pl.multiple_of(c * (FB // 2), FB // 2), FB // 2)
    fetches[3].wait()
    fetches[4].wait()
    fetches[5].wait()
    for yy in range(Y):
        wcat[mine_rows, yy * HD:(yy + 1) * HD] = hout[:, pl.ds(pl.multiple_of((2 * yy + c) * HD, HD), HD)]
    if X > 1:
        drain(planes.at[:, pl.ds(0, X - 1)], s0r)

    fan = NY * Z * 2

    def route(i, _):
        n = lax.rem(i + 2 * z + c, fan)
        yi = n // (2 * Z)
        zt = (n // 2) % Z
        ct = n % 2
        st = seq_of(zt, (yi * X + x + Y - ct * (Y // 2)) % Y, ct)

        @pl.when(st != s)
        def _():
            send(planes.at[yi, zt // 2, zt % 2, ct], landed.at[s], s1s, s1r, (st, x))

        return 0

    lax.fori_loop(0, fan, route, 0)

    @pl.when(handler)
    def _():
        landed[pl.ds(s, 1)] = planes[
            pl.ds(unit // X, 1), pl.ds(z // 2, 1), pl.ds(z % 2, 1), pl.ds(c, 1)
        ].reshape(1, slots, FB)

    th = T // 2
    front, back = pl.ds(0, th), pl.ds(th, th)
    if X > 2:
        send(tok.at[front], tall.at[x, front], tks.at[0], tkr.at[0], (s, right))
        send(tok.at[back], tall.at[x, back], tks.at[1], tkr.at[1], (s, left))
    elif X > 1:
        send(tok, tall.at[x], tks.at[0], tkr.at[0], (s, right))

    j = 2 * y + c

    def weights_out(i, _):
        jt = lax.rem(j + 1 + i, nb)
        yt = jt // 2
        ct = jt % 2
        cols = pl.ds(pl.multiple_of(yt * 2 * HD, 2 * HD), 2 * HD)

        @pl.when(ct == 0)
        def _():
            send(hin.at[pl.ds(0, 1), :, cols], wbuf.at[pl.ds(0, 1), j], wss, wsr, (seq_of(z, yt, ct), x))

        @pl.when(ct == 1)
        def _():
            send(hin.at[pl.ds(1, 2), :, cols], wbuf.at[pl.ds(0, 2), j], wss, wsr, (seq_of(z, yt, ct), x))

        return 0

    lax.fori_loop(0, nb - 1, weights_out, 0)
    own_cols = pl.ds(pl.multiple_of(y * 2 * HD, 2 * HD), 2 * HD)

    @pl.when(c == 0)
    def _():
        wbuf[pl.ds(0, 1), pl.ds(j, 1)] = hin[pl.ds(0, 1), :, own_cols].reshape(1, 1, hin.shape[1], 2 * HD)

    @pl.when(c == 1)
    def _():
        wbuf[pl.ds(0, 2), pl.ds(j, 1)] = hin[pl.ds(1, 2), :, own_cols].reshape(2, 1, hin.shape[1], 2 * HD)

    for yy in range(Y):
        theirs = pl.ds(pl.multiple_of((2 * yy + 1 - c) * HD, HD), HD)
        send(hout.at[:, theirs], wcat.at[mine_rows, pl.ds(yy * HD, HD)], wos, wor, twin)

    q_idx = compact_index(qtab[...])
    c_idx = compact_index(ctab[...])
    krows = q_idx.shape[0]

    @pl.when(handler)
    def _():
        mine = jnp.where(c == 0, q_idx, c_idx)
        row_id = iota((R, 128), 0).astype(F32)
        for k in range(krows):
            comp[:, k * 128:(k + 1) * 128] = onehot(row_id == mine[k:k + 1, :])

    rq = R // 4
    quarters = [pl.ds(i * rq, rq) for i in range(4)]
    turns = (0, 2, 1, 3)
    lower, upper = pl.ds(0, R // 2), pl.ds(R // 2, R // 2)

    def to_row(q, u, k):
        for d in range(1, X):
            send(xall.at[u, quarters[q]], xall.at[u, quarters[q]], xs.at[k], xr.at[k], (s, lax.rem(x + d, X)))

    def to_column(q, u, k):
        for d in range(1, Y):
            to = (seq_of(z, lax.rem(y + d, Y), c), x)
            send(xall.at[u, quarters[q]], xall.at[u, quarters[q]], xs.at[k], xr.at[k], to)

    @pl.when(handler)
    def _():
        drain(landed.at[pl.ds(0, S - 1)], s1r)
        for q in turns:
            xall[pl.ds(unit, 1), quarters[q]] = dot(
                comp[quarters[q], :], landed[...].reshape(S * slots, FB)
            ).astype(BF).reshape(1, rq, FB)
            if q < 2:
                to_row(q, unit, q)
                to_column(q, unit, 4)
            else:
                to_column(q, unit, q)
                if NY == 1:
                    to_row(q, unit, 5)

    cidx[...] = q_idx
    half = krows // 2
    per_z = krows // Z

    def back_row(k):
        ahead = jnp.where(c == 0, Z // 2 - 1 - k // per_z, Z // 2 + k // per_z)
        return lax.rem(z + ahead, Z) * per_z + lax.rem(k + y, per_z)

    col_id = iota((128, R), 1).astype(F32)
    for k in range(half):
        column = as_column(cidx[pl.ds(back_row(k), 1), :])
        sel[k * 128:(k + 1) * 128, :] = onehot(column == col_id)

    for q in turns:
        if q < 2:
            @pl.when(jnp.logical_not(handler))
            def _():
                drain(xall.at[0, quarters[q]], xr.at[q])
                to_column(q, unit, 4)
        elif NY == 1:
            @pl.when(jnp.logical_not(handler))
            def _():
                drain(xall.at[0, quarters[q]], xr.at[q])
                to_row(q, x, 5)
        else:
            @pl.when(handler)
            def _():
                drain(xall.at[pl.ds(0, NY - 1), quarters[q]], xr.at[q])

            @pl.when(jnp.logical_not(handler))
            def _():
                drain(xall.at[pl.ds(0, NY), quarters[q]], xr.at[q])

            for i in range(NY):
                to_row(q, i * X + x, 5)

    if X > 2:
        drain(tall.at[0, front], tkr.at[0])
        send(tall.at[left, front], tall.at[left, front], tks.at[2], tkr.at[2], (s, right))
        drain(tall.at[0, back], tkr.at[1])
        send(tall.at[right, back], tall.at[right, back], tks.at[3], tkr.at[3], (s, left))
        send(tok.at[back], tall.at[x, back], tks.at[4], tkr.at[4], (s, right))
        send(tok.at[front], tall.at[x, front], tks.at[5], tkr.at[5], (s, left))
    elif X > 1:
        drain(tall.at[0], tkr.at[0])

    @pl.when(c == 0)
    def _():
        drain(wbuf.at[pl.ds(0, 1), pl.ds(0, nb - 1)], wsr)

    @pl.when(c == 1)
    def _():
        drain(wbuf.at[pl.ds(0, 2), pl.ds(0, nb - 1)], wsr)

    if Y > 1:
        drain(xall.at[pl.ds(0, Y - 1), lower], xr.at[4])
    if X > 1:
        drain(xall.at[pl.ds(0, NY * (X - 1)), upper], xr.at[5])

    def projected(i):
        total = None
        for yy in range(Y):
            term = dot(xall[yy], wbuf[i, 2 * yy:2 * yy + 2].reshape(FB, 2 * HD))
            total = term if total is None else total + term
        part[:, i] = total.astype(BF).reshape(Z, rz, 2 * HD)

    def sum_out(i):
        projected(i)
        for d in others:
            zt = lax.rem(z + d, Z)
            send(part.at[zt, i], rsum.at[z, i], rs.at[i], rr.at[i], (seq_of(zt, y, c), x))
        rsum[pl.ds(z, 1), i:i + 1] = part[pl.ds(z, 1), i:i + 1]

    sum_out(0)

    @pl.when(c == 1)
    def _():
        sum_out(1)

    load_in.wait()

    def project_light(source, at, first):
        def one(i, _):
            term = dot(source[...], lw[i, pl.ds(pl.multiple_of(at * FX, FX), FX), :])
            if first:
                lmap[i] = term
            else:
                lmap[i] += term
            return 0

        lax.fori_loop(0, 3, one, 0)

    project_light(tok, x, True)

    def summed(i):
        drain(rsum.at[pl.ds(0, Z - 1), 0], rr.at[i])
        return jnp.sum(rsum[:, i].astype(F32), axis=0).astype(BF)

    def kv_out(i):
        total = summed(i)
        for g in range(2):
            kv[g, i, pl.ds(z, 1)] = total[:, g * HD:(g + 1) * HD].reshape(1, rz, HD)
        for d in [*others, 0]:
            zt = lax.rem(z + d, Z)
            send(kv.at[0, i, z], kv.at[1, i, z], kvs.at[i], kvr.at[i], (seq_of(zt, y, 0), x))
            if d:
                send(kv.at[1, i, z], kv.at[1, i, z], kvs.at[i], kvr.at[i], (seq_of(zt, y, 1), x))

    @pl.when(c == 0)
    def _():
        total = summed(0)
        qbuf[0] = total[:, :HD]
        qbuf[1] = total[:, HD:]
        send(qbuf.at[1], qbuf.at[0], qs, qr, twin)

    @pl.when(c == 1)
    def _():
        kv_out(0)
        kv_out(1)

    if X > 2:
        drain(tall.at[0, front], tkr.at[2])
        drain(tall.at[0, back], tkr.at[3])
        drain(tall.at[0, back], tkr.at[4])
        drain(tall.at[0, front], tkr.at[5])
    if X > 1:
        project_light(tall.at[left], left, False)
    if X > 2:
        project_light(tall.at[right], right, False)
        project_light(tall.at[far], far, False)

    for g in range(2):
        for blk in range(T // LB):
            rows = slice(blk * LB, (blk + 1) * LB)
            cols = slice(g * HD, (g + 1) * HD)
            lheads[rows, cols] = softmax_value(
                lmap[0, rows, cols].astype(BF), lmap[1, rows, cols].astype(BF), lmap[2, rows, cols].astype(BF)
            )
    load_out.wait()

    def light_out(xt):
        return dot(lheads[...], lo[:, pl.ds(pl.multiple_of(xt * FX, FX), FX)])

    if X > 2:
        lsend[2] = light_out(far).astype(BF)
        send(lsend.at[2, front], lfar.at[0], lrs, lfr.at[0], (s, right))
        send(lsend.at[2, back], lfar.at[1], lrs, lfr.at[1], (s, left))
    if X > 1:
        lsend[0] = light_out(right).astype(BF)
    if X > 2:
        send(lsend.at[0, back], lrecv.at[0, back], lrs, lrr, (s, right))
        lsend[1] = light_out(left).astype(BF)
        send(lsend.at[1, front], lrecv.at[1, front], lrs, lrr, (s, left))
    elif X > 1:
        send(lsend.at[0], lrecv.at[0], lrs, lrr, (s, right))

    def arrived(i):
        @pl.when(c == 0)
        def _():
            drain(kv.at[1, 0], kvr.at[i])

        @pl.when(c == 1)
        def _():
            drain(kv.at[1, 0, pl.ds(0, Z - 1)], kvr.at[i])

    @pl.when(c == 1)
    def _():
        drain(qbuf.at[0], qr)

    arrived(0)
    scores = dot_nt(qbuf[0], kv[1, 0].reshape(R, HD)) * (1.0 / math.sqrt(HD))
    expanded = jnp.exp(scores - jnp.max(scores, axis=-1, keepdims=True))
    totals = jnp.sum(expanded, axis=-1, keepdims=True)
    arrived(1)
    heads = (dot(expanded.astype(BF), kv[1, 1].reshape(R, HD)) / totals).astype(BF)
    oy[pl.ds(y, 1), pl.ds(z, 1)] = heads.reshape(1, 1, rz, HD)
    for d in others:
        zt = lax.rem(z + d, Z)
        send(oy.at[y, z], oy.at[y, z], ozs, ozr.at[d], (seq_of(zt, y, c), x))

    def heads_over_y(zz):
        for d in range(1, Y):
            send(oy.at[y, zz], oy.at[y, zz], oys, oyr, (seq_of(z, lax.rem(y + d, Y), c), x))

    heads_over_y(z)
    lacc[...] = light_out(x)
    for d in reversed(others):
        drain(oy.at[0, 0], ozr.at[d])
        heads_over_y(lax.rem(z + Z - d, Z))

    if X > 2:
        drain(lfar.at[0], lfr.at[0])
        lsend[0, :th] = (lsend[0, :th].astype(F32) + lfar[0].astype(F32)).astype(BF)
        send(lsend.at[0, front], lrecv.at[0, front], lrs, lrr, (s, right))
        drain(lfar.at[1], lfr.at[1])
        lsend[1, th:] = (lsend[1, th:].astype(F32) + lfar[1].astype(F32)).astype(BF)
        send(lsend.at[1, back], lrecv.at[1, back], lrs, lrr, (s, left))

    drain(wcat.at[pl.ds(0, FB // 2)], wor)
    if Y > 1:
        drain(oy.at[pl.ds(0, Y - 1)], oyr)
    total = None
    for yy in range(Y):
        term = dot_nt(oy[yy].reshape(R, HD), wcat[:, yy * HD:(yy + 1) * HD])
        total = term if total is None else total + term
    rmine[...] = total.astype(BF)
    send(rmine, rother, cs, cr, twin)
    drain(rother, cr)
    drain(rmine, cs)
    both = (total + rother[...].astype(F32)).astype(BF)
    rmine[...] = both

    block = pl.ds(pl.multiple_of(((z % 2) * Y + y) * FB, FB), FB)
    xq = z // 2

    step = S // 2 // half

    def choose(k, _):
        chosen = dot(sel[pl.ds(pl.multiple_of(k * 128, 128), 128), :], rmine[...]).astype(BF)
        rsel[pl.ds(k * step, step)] = chosen.reshape(step, slots, FB)
        for i in range(step):
            st = back_row(k) * step + i
            here = jnp.logical_and(st == s, xq == x)

            @pl.when(jnp.logical_not(here))
            def _():
                send(rsel.at[k * step + i], ret.at[x, :, block], rts, rtr, (st, xq))

            @pl.when(here)
            def _():
                ret[pl.ds(x, 1), :, block] = rsel[pl.ds(k * step + i, 1)]

        return 0

    lax.fori_loop(0, half, choose, 0)
    keeps = jnp.logical_and(xq == x, c == 0)

    if X > 2:
        drain(lrecv, lrr)
        lacc[...] = lacc[...] + lrecv[0].astype(F32) + lrecv[1].astype(F32)
    elif X > 1:
        drain(lrecv.at[0], lrr)
        lacc[...] = lacc[...] + lrecv[0].astype(F32)
    onto = onehot(as_row(own_q) == iota((T, slots), 0).astype(F32))
    gates = as_column(gate[...])

    @pl.when(keeps)
    def _():
        drain(landed.at[pl.ds(0, nb * X - 1)], rtr)

    @pl.when(jnp.logical_not(keeps))
    def _():
        drain(landed.at[pl.ds(0, nb * X)], rtr)

    update = jnp.sum(ret[...].astype(F32), axis=0) * gates
    high = update.astype(BF)
    low = (update - high.astype(F32)).astype(BF)
    out[...] = (lacc[...] + dot(onto, high) + dot(onto, low)).astype(BF)

    if X > 1:
        drain(planes.at[:, pl.ds(0, X - 1)], s0s)
        drain(xall.at[pl.ds(0, NY * (X - 1)), upper], xs.at[5])
        drain(tall.at[0, front] if X > 2 else tall.at[0], tks.at[0])

    @pl.when(handler)
    def _():
        drain(landed.at[pl.ds(0, fan - 1)], s1s)
        if X > 1:
            for q in range(2):
                drain(xall.at[pl.ds(0, X - 1), quarters[q]], xs.at[q])
        if Y > 1:
            for q in range(2, 4):
                drain(xall.at[pl.ds(0, Y - 1), quarters[q]], xs.at[q])

    @pl.when(jnp.logical_not(handler))
    def _():
        drain(landed.at[pl.ds(0, fan)], s1s)

    @pl.when(c == 0)
    def _():
        if Y > 1:
            drain(wbuf.at[pl.ds(0, 1), pl.ds(0, Y - 1)], wss)
        drain(wbuf.at[pl.ds(0, 2), pl.ds(0, Y)], wss)

    @pl.when(c == 1)
    def _():
        drain(wbuf.at[pl.ds(0, 1), pl.ds(0, Y)], wss)
        if Y > 1:
            drain(wbuf.at[pl.ds(0, 2), pl.ds(0, Y - 1)], wss)

    drain(wcat.at[pl.ds(0, FB // 2)], wos)
    if X > 2:
        drain(tall.at[0, back], tks.at[1])
        drain(tall.at[0, back], tks.at[4])
        drain(tall.at[0, front], tks.at[5])
        drain(tall.at[0, front], tks.at[2])
        drain(tall.at[0, back], tks.at[3])
        drain(lsend, lrs)
    elif X > 1:
        drain(lsend.at[0], lrs)
    if Y > 1:
        drain(xall.at[pl.ds(0, Y - 1), lower], xs.at[4])
        drain(oy.at[pl.ds(0, Y - 1)], oys)

    drain(rsum.at[pl.ds(0, Z - 1), 0], rs.at[0])

    @pl.when(c == 0)
    def _():
        drain(qbuf.at[0], qs)

    @pl.when(c == 1)
    def _():
        drain(rsum.at[pl.ds(0, Z - 1), 0], rs.at[1])
        for i in range(2):
            drain(kv.at[0, 0], kvs.at[i])
            drain(kv.at[0, 0, pl.ds(0, Z - 1)], kvs.at[i])

    drain(oy.at[0, pl.ds(0, Z - 1)], ozs)

    @pl.when(keeps)
    def _():
        drain(rsel.at[pl.ds(0, S // 2 - 1)], rts)

    @pl.when(jnp.logical_not(keeps))
    def _():
        drain(rsel, rts)


def body(dims, tokens, light_input, light_output, heavy_input, heavy_output, query_tokens, context_tokens, query_gate):
    Z, Y, X = dims
    S = Z * Y * 2
    nb = 2 * Y
    slots = query_tokens.shape[1]
    T, FX = tokens.shape
    R = S * T // 32
    rz = R // Z
    D = light_input.shape[1]
    LX = light_input.shape[2]
    hbm = pl.BlockSpec(memory_space=pl.ANY)
    dma = pltpu.SemaphoreType.DMA
    scratch = [
        pltpu.VMEM((T, FX), BF),
        pltpu.VMEM(heavy_input.shape, BF),
        pltpu.VMEM((FB // 2, 2 * Y * HD), BF),
        pltpu.VMEM((slots, S), jnp.int32),
        pltpu.VMEM((slots, S), jnp.int32),
        pltpu.VMEM((1, slots), F32),
        pltpu.VMEM((Y, 2, 2, slots, FB), BF),
        pltpu.VMEM((Y // X, X, 2, 2, slots, FB), BF),
        pltpu.VMEM((S, slots, FB), BF),
        pltpu.VMEM((R, S * slots), BF),
        pltpu.VMEM((S * slots // 2, R), BF),
        pltpu.VMEM((Y, R, FB), BF),
        pltpu.VMEM((2, nb, FB // 2, 2 * HD), BF),
        pltpu.VMEM((Z, 2, rz, 2 * HD), BF),
        pltpu.VMEM((Z, 2, rz, 2 * HD), BF),
        pltpu.VMEM((2, 2, Z, rz, HD), BF),
        pltpu.VMEM((2, rz, HD), BF),
        pltpu.VMEM((Y, Z, rz, HD), BF),
        pltpu.VMEM((FB, Y * HD), BF),
        pltpu.VMEM((R, FB), BF),
        pltpu.VMEM((R, FB), BF),
        pltpu.VMEM((S // 2, slots, FB), BF),
        pltpu.VMEM((X, slots, FX), BF),
        pltpu.VMEM((X, T, FX), BF),
        pltpu.VMEM((3, D, LX), BF),
        pltpu.VMEM((LX, D), BF),
        pltpu.VMEM((3, T, LX), F32),
        pltpu.VMEM((T, LX), BF),
        pltpu.VMEM((3, T, FX), BF),
        pltpu.VMEM((2, T // 2, FX), BF),
        pltpu.VMEM((2, T, FX), BF),
        pltpu.VMEM((T, FX), F32),
        pltpu.VMEM((S * slots // 128, 128), F32),
        *[dma(()) for _ in range(21)],
        dma((6,)), dma((6,)), dma((6,)), dma((6,)), dma((2,)), dma((6,)),
        dma((2,)), dma((2,)), dma((2,)), dma((2,)), dma((Z,)),
    ]
    return pl.pallas_call(
        functools.partial(kernel, dims),
        out_shape=jax.ShapeDtypeStruct((T, FX), BF),
        in_specs=[hbm] * 8,
        out_specs=pl.BlockSpec(memory_space=pltpu.VMEM),
        scratch_shapes=scratch,
        compiler_params=pltpu.CompilerParams(collective_id=0, has_side_effects=True, vmem_limit_bytes=48 << 20),
    )(*(
        pltpu.with_memory_space_constraint(a, pltpu.HBM)
        for a in (
            tokens, light_input, light_output, heavy_input, heavy_output.T, query_tokens.T, context_tokens.T, query_gate
        )
    ))


def solution(mesh):
    X = mesh.shape["head"]
    Z = 2 * X
    dims = (Z, mesh.shape["seq"] // (2 * Z), X)
    placed = (
        P("seq", "head"),
        P(None, None, "head"),
        P("head", None),
        P(None, "seq", "head"),
        P("head", "seq"),
        P(),
        P(),
        P("seq", None),
    )
    return jax.shard_map(
        functools.partial(body, dims), mesh=mesh, in_specs=placed, out_specs=P("seq", "head"), check_vma=False
    )
```

```python
import functools
import math

import jax
import jax.numpy as jnp
from jax import lax
from jax.experimental import pallas as pl
from jax.experimental.pallas import tpu as pltpu
from jax.sharding import PartitionSpec as P

HD = 128
LB = 128
FB = 128
BF = jnp.bfloat16
F32 = jnp.float32


def dot(a, b):
    return jnp.dot(a, b, preferred_element_type=F32)


def dot_nt(a, b):
    return lax.dot_general(a, b, (((1,), (1,)), ((), ())), preferred_element_type=F32)


def iota(shape, dim):
    return lax.broadcasted_iota(jnp.int32, shape, dim)


def as_column(row):
    n = row.shape[1]
    wide = jnp.broadcast_to(row, (n, n))
    return jnp.sum(jnp.where(iota((n, n), 0) == iota((n, n), 1), wide, 0.0), axis=1, keepdims=True)


def as_row(column):
    n = column.shape[0]
    wide = jnp.broadcast_to(column, (n, n))
    return jnp.sum(jnp.where(iota((n, n), 0) == iota((n, n), 1), wide, 0.0), axis=0, keepdims=True)


def onehot(hit):
    return jnp.where(hit, 1.0, 0.0).astype(BF)


def compact_index(table):
    slots, shards = table.shape
    per = 128 // slots
    rows = shards // per
    spread = onehot(iota((128, slots), 0) % slots == iota((128, slots), 1))
    tiled = dot(spread, table.astype(F32).astype(BF))
    keep = iota((128, shards), 1) % per == iota((128, shards), 0) // slots
    join = onehot(iota((rows, shards), 1) // per == iota((rows, shards), 0))
    flat = dot_nt(join, jnp.where(keep, tiled, 0.0).astype(BF))
    live = flat >= 0.0
    marks = onehot(live)
    before = dot(marks, onehot(iota((128, 128), 0) < iota((128, 128), 1)))
    in_row = dot(marks, jnp.ones((128, 128), BF))
    above = dot(onehot(iota((rows, rows), 1) < iota((rows, rows), 0)), in_row.astype(BF))
    return jnp.where(live, before + above, -1.0)


def softmax_value(q, k, v):
    scores = dot_nt(q, k) * (1.0 / math.sqrt(HD))
    expanded = jnp.exp(scores - jnp.max(scores, axis=-1, keepdims=True))
    totals = jnp.sum(expanded, axis=-1, keepdims=True)
    return (dot(expanded.astype(BF), v) / totals).astype(BF)


def kernel(
    dims,
    tok_any, lin, lout, hin_any, hout_any, qtab_any, ctab_any, gate_any,
    out,
    tok, hin, hout, qtab, ctab, gate,
    picks, planes, landed, comp, sel, xall, wbuf, part, rsum, kv, qbuf, hmine, oh,
    wy, psend, precv, rfull, rsel, ret,
    tall, lw, lo, lmap, lheads, lsend, lfar, lrecv, lacc, cidx,
    s0s, s0r, s1s, s1r, wss, wsr, wos, wor, qs, qr,
    ozs, oys, oyr, cs, cr, rts, rtr, lrs, lrr, lis, los,
    tks, tkr, xs, xr, lfr, ins, rs, rr, kvs, kvr, ozr,
):
    Z, Y, X = dims
    NY = Y // X
    nb = 2 * Y
    S = Z * Y * 2
    R = comp.shape[0]
    rz = R // Z
    slots = qtab.shape[0]
    T = tok.shape[0]
    FX = tok.shape[1]
    s = lax.axis_index("seq")
    x = lax.axis_index("head")
    z = s // (2 * Y)
    y = (s // 2) % Y
    c = s % 2
    right, left = lax.rem(x + 1, X), lax.rem(x + X - 1, X)
    far = lax.rem(x + 2, X)

    def seq_of(zz, yy, cc):
        return (zz * Y + yy) * 2 + cc

    twin = (seq_of(z, y, 1 - c), x)
    others = sorted(range(1, Z), key=lambda d: -min(d, Z - d))

    def send(src, dst, ss, rsem, to):
        pltpu.make_async_remote_copy(
            src_ref=src, dst_ref=dst, send_sem=ss, recv_sem=rsem,
            device_id=to, device_id_type=pl.DeviceIdType.MESH,
        ).start()

    def drain(ref, sem):
        pltpu.make_async_copy(ref, ref, sem).wait()

    fetches = [
        pltpu.make_async_copy(src, dst, ins.at[i])
        for i, (src, dst) in enumerate((
            (qtab_any, qtab), (ctab_any, ctab), (tok_any, tok), (hin_any, hin), (hout_any, hout), (gate_any, gate),
        ))
    ]
    for fetch in fetches:
        fetch.start()
    load_in = pltpu.make_async_copy(lin, lw, lis)
    load_out = pltpu.make_async_copy(lout, lo, los)
    barrier = pltpu.get_barrier_semaphore()

    def greet(to):
        pl.semaphore_signal(barrier, inc=1, device_id=to, device_id_type=pl.DeviceIdType.MESH)

    unit = (y + c * (Y // 2)) % Y
    handler = unit % X == x
    zh = Z // 2
    zi = z % zh
    keeper = z // zh
    owns = keeper == c

    for d in range(1, nb):
        jt = lax.rem(2 * y + c + d, nb)
        greet((seq_of(z, jt // 2, jt % 2), x))
    for d in range(1, X):
        greet((s, lax.rem(x + d, X)))

    @pl.when(handler)
    def _():
        def greet_plane(i, _):
            greet((lax.rem(s + 1 + i, S), x))
            return 0

        lax.fori_loop(0, S - 1, greet_plane, 0)

    fetches[0].wait()
    fetches[1].wait()
    here_s = iota((slots, S), 1) == s
    own_q = jnp.sum(jnp.where(here_s, qtab[...].astype(F32), 0.0), axis=1, keepdims=True)
    own_c = jnp.sum(jnp.where(here_s, ctab[...].astype(F32), 0.0), axis=1, keepdims=True)
    fetches[2].wait()
    for i, column in enumerate((own_q, own_c)):
        want = onehot(column == iota((slots, T), 1).astype(F32))
        rows = dot(want, tok[...]).astype(BF)
        for b in range(nb):
            picks[b % Y, b // Y, i] = rows[:, b * FB:(b + 1) * FB]

    met = (nb - 1) + (X - 1) + NY * Z * 2

    @pl.when(handler)
    def _():
        pl.semaphore_wait(barrier, met - 1)

    @pl.when(jnp.logical_not(handler))
    def _():
        pl.semaphore_wait(barrier, met)

    for d in range(1, X):
        xt = lax.rem(x + d, X)
        for i in range(NY):
            send(picks.at[i * X + xt], planes.at[i, x], s0s, s0r, (s, xt))
    for i in range(NY):
        planes[i, pl.ds(x, 1)] = picks[pl.ds(i * X + x, 1)]

    fetches[3].wait()
    fetches[4].wait()
    fetches[5].wait()
    if X > 1:
        drain(planes.at[:, pl.ds(0, X - 1)], s0r)

    fan = NY * Z * 2

    def route(i, _):
        n = lax.rem(i + 2 * z + c, fan)
        yi = n // (2 * Z)
        zt = (n // 2) % Z
        ct = n % 2
        st = seq_of(zt, (yi * X + x + Y - ct * (Y // 2)) % Y, ct)

        @pl.when(st != s)
        def _():
            send(planes.at[yi, zt // 2, zt % 2, ct], landed.at[s], s1s, s1r, (st, x))

        return 0

    lax.fori_loop(0, fan, route, 0)

    @pl.when(handler)
    def _():
        landed[pl.ds(s, 1)] = planes[
            pl.ds(unit // X, 1), pl.ds(z // 2, 1), pl.ds(z % 2, 1), pl.ds(c, 1)
        ].reshape(1, slots, FB)

    load_in.start()
    load_out.start()

    th = T // 2
    front, back = pl.ds(0, th), pl.ds(th, th)
    if X > 2:
        send(tok.at[front], tall.at[x, front], tks.at[0], tkr.at[0], (s, right))
        send(tok.at[back], tall.at[x, back], tks.at[1], tkr.at[1], (s, left))
    elif X > 1:
        send(tok, tall.at[x], tks.at[0], tkr.at[0], (s, right))

    j = 2 * y + c

    def weights_out(i, _):
        jt = lax.rem(j + 1 + i, nb)
        yt = jt // 2
        ct = jt % 2
        cols = pl.ds(pl.multiple_of(yt * 2 * HD, 2 * HD), 2 * HD)

        @pl.when(ct == 0)
        def _():
            send(hin.at[pl.ds(0, 1), :, cols], wbuf.at[pl.ds(0, 1), j], wss, wsr, (seq_of(z, yt, ct), x))

        @pl.when(ct == 1)
        def _():
            send(hin.at[pl.ds(1, 2), :, cols], wbuf.at[pl.ds(0, 2), j], wss, wsr, (seq_of(z, yt, ct), x))

        return 0

    lax.fori_loop(0, nb - 1, weights_out, 0)
    own_cols = pl.ds(pl.multiple_of(y * 2 * HD, 2 * HD), 2 * HD)

    @pl.when(c == 0)
    def _():
        wbuf[pl.ds(0, 1), pl.ds(j, 1)] = hin[pl.ds(0, 1), :, own_cols].reshape(1, 1, hin.shape[1], 2 * HD)

    @pl.when(c == 1)
    def _():
        wbuf[pl.ds(0, 2), pl.ds(j, 1)] = hin[pl.ds(1, 2), :, own_cols].reshape(2, 1, hin.shape[1], 2 * HD)

    wrows = pl.ds(pl.multiple_of(j * (FB // 2), FB // 2), FB // 2)
    for d in range(1, nb):
        jt = lax.rem(j + d, nb)
        cols = pl.ds(pl.multiple_of(jt // 2 * 2 * HD, 2 * HD), 2 * HD)
        send(hout.at[:, cols], wy.at[wrows, :], wos, wor, (seq_of(z, jt // 2, jt % 2), x))
    wy[wrows, :] = hout[:, own_cols]

    q_idx = compact_index(qtab[...])
    c_idx = compact_index(ctab[...])
    krows = q_idx.shape[0]

    @pl.when(handler)
    def _():
        mine = jnp.where(c == 0, q_idx, c_idx)
        row_id = iota((R, 128), 0).astype(F32)
        for k in range(krows):
            comp[:, k * 128:(k + 1) * 128] = onehot(row_id == mine[k:k + 1, :])

    rq = R // 4
    rt = rq // Z
    quarters = [pl.ds(i * rq, rq) for i in range(4)]
    turns = (0, 2, 1, 3)

    def to_row(q, u, k):
        for d in range(1, X):
            send(xall.at[u, quarters[q]], xall.at[u, quarters[q]], xs.at[k], xr.at[k], (s, lax.rem(x + d, X)))

    def to_column(q, u, k):
        for d in range(1, Y):
            to = (seq_of(z, lax.rem(y + d, Y), c), x)
            send(xall.at[u, quarters[q]], xall.at[u, quarters[q]], xs.at[k], xr.at[k], to)

    @pl.when(handler)
    def _():
        drain(landed.at[pl.ds(0, S - 1)], s1r)
        for q in turns:
            xall[pl.ds(unit, 1), quarters[q]] = dot(
                comp[quarters[q], :], landed[...].reshape(S * slots, FB)
            ).astype(BF).reshape(1, rq, FB)
            if q < 2:
                to_row(q, unit, q)
                to_column(q, unit, 4 + q)
            else:
                to_column(q, unit, q)
                if NY == 1:
                    to_row(q, unit, 4 + q)

    cidx[...] = q_idx
    half = krows // 2
    per_z = krows // Z

    def back_row(k):
        ahead = jnp.where(c == 0, Z // 2 - 1 - k // per_z, Z // 2 + k // per_z)
        return lax.rem(z + ahead, Z) * per_z + lax.rem(k + y, per_z)

    held = iota((128, R), 1)
    place = held % rz // rt
    quarter = jnp.where(place == 1, 2, jnp.where(place == 2, 1, place))
    col_id = (quarter * rq + held // rz * rt + held % rt).astype(F32)
    for k in range(half):
        column = as_column(cidx[pl.ds(back_row(k), 1), :])
        sel[k * 128:(k + 1) * 128, :] = onehot(column == col_id)

    for q in turns:
        if q < 2:
            @pl.when(jnp.logical_not(handler))
            def _():
                drain(xall.at[0, quarters[q]], xr.at[q])
                to_column(q, unit, 4 + q)
        elif NY == 1:
            @pl.when(jnp.logical_not(handler))
            def _():
                drain(xall.at[0, quarters[q]], xr.at[q])
                to_row(q, x, 4 + q)
        else:
            @pl.when(handler)
            def _():
                drain(xall.at[pl.ds(0, NY - 1), quarters[q]], xr.at[q])

            @pl.when(jnp.logical_not(handler))
            def _():
                drain(xall.at[pl.ds(0, NY), quarters[q]], xr.at[q])

            for i in range(NY):
                to_row(q, i * X + x, 4 + q)

    if X > 2:
        drain(tall.at[0, front], tkr.at[0])
        send(tall.at[left, front], tall.at[left, front], tks.at[2], tkr.at[2], (s, right))
        drain(tall.at[0, back], tkr.at[1])
        send(tall.at[right, back], tall.at[right, back], tks.at[3], tkr.at[3], (s, left))
        send(tok.at[back], tall.at[x, back], tks.at[4], tkr.at[4], (s, right))
        send(tok.at[front], tall.at[x, front], tks.at[5], tkr.at[5], (s, left))
    elif X > 1:
        drain(tall.at[0], tkr.at[0])

    @pl.when(c == 0)
    def _():
        drain(wbuf.at[pl.ds(0, 1), pl.ds(0, nb - 1)], wsr)

    @pl.when(c == 1)
    def _():
        drain(wbuf.at[pl.ds(0, 2), pl.ds(0, nb - 1)], wsr)

    def there(q):
        if q < 2 and Y > 1:
            drain(xall.at[pl.ds(0, Y - 1), quarters[q]], xr.at[4 + q])
        if q >= 2 and X > 1:
            drain(xall.at[pl.ds(0, NY * (X - 1)), quarters[q]], xr.at[4 + q])

    def projected(i, at):
        total = None
        for yy in range(Y):
            term = dot(xall[yy, quarters[turns[at]]], wbuf[i, 2 * yy:2 * yy + 2].reshape(FB, 2 * HD))
            total = term if total is None else total + term
        part[:, i, at * rt:(at + 1) * rt] = total.astype(BF).reshape(Z, rt, 2 * HD)

    def sum_out(i, first, last):
        rows = pl.ds(first * rt, (last - first) * rt)
        for at in range(first, last):
            projected(i, at)
        for d in others:
            zt = lax.rem(z + d, Z)
            send(part.at[zt, i, rows], rsum.at[z, i, rows], rs.at[i], rr.at[i], (seq_of(zt, y, c), x))

    for h in range(2):
        there(turns[2 * h])
        there(turns[2 * h + 1])
        sum_out(0, 2 * h, 2 * h + 2)

    @pl.when(c == 1)
    def _():
        sum_out(1, 0, 4)

    rsum[pl.ds(z, 1), 0:1] = part[pl.ds(z, 1), 0:1]

    @pl.when(c == 1)
    def _():
        rsum[pl.ds(z, 1), 1:2] = part[pl.ds(z, 1), 1:2]

    load_in.wait()

    def project_light(source, at, first):
        def one(i, _):
            term = dot(source[...], lw[i, pl.ds(pl.multiple_of(at * FX, FX), FX), :])
            if first:
                lmap[i] = term
            else:
                lmap[i] += term
            return 0

        lax.fori_loop(0, 3, one, 0)

    project_light(tok, x, True)

    def summed(i):
        drain(rsum.at[pl.ds(0, Z - 1), 0], rr.at[i])
        return jnp.sum(rsum[:, i].astype(F32), axis=0).astype(BF)

    def kv_out(i):
        total = summed(i)
        for g in range(2):
            kv[g, i, pl.ds(z, 1)] = total[:, g * HD:(g + 1) * HD].reshape(1, rz, HD)
        for d in [*others, 0]:
            zt = lax.rem(z + d, Z)
            send(kv.at[0, i, z], kv.at[1, i, z], kvs.at[i], kvr.at[i], (seq_of(zt, y, 0), x))
            if d:
                send(kv.at[1, i, z], kv.at[1, i, z], kvs.at[i], kvr.at[i], (seq_of(zt, y, 1), x))

    @pl.when(c == 0)
    def _():
        total = summed(0)
        qbuf[0] = total[:, :HD]
        qbuf[1] = total[:, HD:]
        send(qbuf.at[1], qbuf.at[0], qs, qr, twin)

    @pl.when(c == 1)
    def _():
        kv_out(0)
        kv_out(1)

    if X > 2:
        drain(tall.at[0, front], tkr.at[2])
        drain(tall.at[0, back], tkr.at[3])
        drain(tall.at[0, back], tkr.at[4])
        drain(tall.at[0, front], tkr.at[5])
    if X > 1:
        project_light(tall.at[left], left, False)
    if X > 2:
        project_light(tall.at[right], right, False)
        project_light(tall.at[far], far, False)

    for g in range(2):
        for blk in range(T // LB):
            rows = slice(blk * LB, (blk + 1) * LB)
            cols = slice(g * HD, (g + 1) * HD)
            lheads[rows, cols] = softmax_value(
                lmap[0, rows, cols].astype(BF), lmap[1, rows, cols].astype(BF), lmap[2, rows, cols].astype(BF)
            )
    load_out.wait()

    def light_out(xt):
        return dot(lheads[...], lo[:, pl.ds(pl.multiple_of(xt * FX, FX), FX)])

    if X > 2:
        lsend[2] = light_out(far).astype(BF)
        send(lsend.at[2, front], lfar.at[0], lrs, lfr.at[0], (s, right))
        send(lsend.at[2, back], lfar.at[1], lrs, lfr.at[1], (s, left))
    if X > 1:
        lsend[0] = light_out(right).astype(BF)
    if X > 2:
        send(lsend.at[0, back], lrecv.at[0, back], lrs, lrr, (s, right))
        lsend[1] = light_out(left).astype(BF)
        send(lsend.at[1, front], lrecv.at[1, front], lrs, lrr, (s, left))
    elif X > 1:
        send(lsend.at[0], lrecv.at[0], lrs, lrr, (s, right))

    def arrived(i):
        @pl.when(c == 0)
        def _():
            drain(kv.at[1, 0], kvr.at[i])

        @pl.when(c == 1)
        def _():
            drain(kv.at[1, 0, pl.ds(0, Z - 1)], kvr.at[i])

    @pl.when(c == 1)
    def _():
        drain(qbuf.at[0], qr)

    arrived(0)
    scores = dot_nt(qbuf[0], kv[1, 0].reshape(R, HD)) * (1.0 / math.sqrt(HD))
    expanded = jnp.exp(scores - jnp.max(scores, axis=-1, keepdims=True))
    totals = jnp.sum(expanded, axis=-1, keepdims=True)
    arrived(1)
    heads = (dot(expanded.astype(BF), kv[1, 1].reshape(R, HD)) / totals).astype(BF)
    heads_at = (pl.ds(pl.multiple_of(zi * rz, rz), rz), pl.ds(pl.multiple_of(c * HD, HD), HD))
    hmine[...] = heads

    @pl.when(owns)
    def _():
        oh[heads_at] = heads

    for d in others:
        send(hmine, oh.at[heads_at], ozs, ozr, (seq_of(lax.rem(z + d, Z), y, keeper), x))

    @pl.when(jnp.logical_not(owns))
    def _():
        send(hmine, oh.at[heads_at], ozs, ozr, twin)

    lacc[...] = light_out(x)
    drain(wy.at[pl.ds(0, (nb - 1) * (FB // 2))], wor)

    @pl.when(owns)
    def _():
        drain(rsel.at[pl.ds(0, (Z - 1) * rz // slots)], ozr)

    @pl.when(jnp.logical_not(owns))
    def _():
        drain(oh, ozr)

    ph = zh * rz // 2
    for h in range(2):
        rows = pl.ds(h * ph, ph)
        product = dot_nt(oh[rows, :], wy[...]).astype(BF)
        for yy in range(Y):
            psend[yy, rows] = product[:, yy * FB:(yy + 1) * FB]
        for d in range(1, Y):
            yt = lax.rem(y + d, Y)
            send(psend.at[yt, rows], precv.at[y, rows], oys, oyr, (seq_of(z, yt, c), x))
        precv[pl.ds(y, 1), rows] = psend[pl.ds(y, 1), rows]

    if X > 2:
        drain(lfar.at[0], lfr.at[0])
        lsend[0, :th] = (lsend[0, :th].astype(F32) + lfar[0].astype(F32)).astype(BF)
        send(lsend.at[0, front], lrecv.at[0, front], lrs, lrr, (s, right))
        drain(lfar.at[1], lfr.at[1])
        lsend[1, th:] = (lsend[1, th:].astype(F32) + lfar[1].astype(F32)).astype(BF)
        send(lsend.at[1, back], lrecv.at[1, back], lrs, lrr, (s, left))

    if Y > 1:
        drain(precv.at[pl.ds(0, Y - 1)], oyr)
    rfull[pl.ds(c, 1)] = jnp.sum(precv[...].astype(F32), axis=0).astype(BF).reshape(1, zh * rz, FB)
    send(rfull.at[c], rfull.at[c], cs, cr, twin)
    drain(rfull.at[0], cr)

    block = pl.ds(pl.multiple_of(((z % 2) * Y + y) * FB, FB), FB)
    xq = z // 2

    step = S // 2 // half

    def choose(k, _):
        chosen = dot(sel[pl.ds(pl.multiple_of(k * 128, 128), 128), :], rfull[...].reshape(R, FB)).astype(BF)
        rsel[pl.ds(k * step, step)] = chosen.reshape(step, slots, FB)
        for i in range(step):
            st = back_row(k) * step + i
            here = jnp.logical_and(st == s, xq == x)

            @pl.when(jnp.logical_not(here))
            def _():
                send(rsel.at[k * step + i], ret.at[x, :, block], rts, rtr, (st, xq))

            @pl.when(here)
            def _():
                ret[pl.ds(x, 1), :, block] = rsel[pl.ds(k * step + i, 1)]

        return 0

    lax.fori_loop(0, half, choose, 0)
    keeps = jnp.logical_and(xq == x, c == 0)

    if X > 2:
        drain(lrecv, lrr)
        lacc[...] = lacc[...] + lrecv[0].astype(F32) + lrecv[1].astype(F32)
    elif X > 1:
        drain(lrecv.at[0], lrr)
        lacc[...] = lacc[...] + lrecv[0].astype(F32)
    onto = onehot(as_row(own_q) == iota((T, slots), 0).astype(F32))
    gates = as_column(gate[...])

    @pl.when(keeps)
    def _():
        drain(landed.at[pl.ds(0, nb * X - 1)], rtr)

    @pl.when(jnp.logical_not(keeps))
    def _():
        drain(landed.at[pl.ds(0, nb * X)], rtr)

    update = jnp.sum(ret[...].astype(F32), axis=0) * gates
    high = update.astype(BF)
    low = (update - high.astype(F32)).astype(BF)
    out[...] = (lacc[...] + dot(onto, high) + dot(onto, low)).astype(BF)

    if X > 1:
        drain(planes.at[:, pl.ds(0, X - 1)], s0s)
        for q in (2, 3):
            drain(xall.at[pl.ds(0, NY * (X - 1)), quarters[q]], xs.at[4 + q])
        drain(tall.at[0, front] if X > 2 else tall.at[0], tks.at[0])

    @pl.when(handler)
    def _():
        drain(landed.at[pl.ds(0, fan - 1)], s1s)
        if X > 1:
            for q in range(2):
                drain(xall.at[pl.ds(0, X - 1), quarters[q]], xs.at[q])
        if Y > 1:
            for q in range(2, 4):
                drain(xall.at[pl.ds(0, Y - 1), quarters[q]], xs.at[q])

    @pl.when(jnp.logical_not(handler))
    def _():
        drain(landed.at[pl.ds(0, fan)], s1s)

    @pl.when(c == 0)
    def _():
        if Y > 1:
            drain(wbuf.at[pl.ds(0, 1), pl.ds(0, Y - 1)], wss)
        drain(wbuf.at[pl.ds(0, 2), pl.ds(0, Y)], wss)

    @pl.when(c == 1)
    def _():
        drain(wbuf.at[pl.ds(0, 1), pl.ds(0, Y)], wss)
        if Y > 1:
            drain(wbuf.at[pl.ds(0, 2), pl.ds(0, Y - 1)], wss)

    drain(wy.at[pl.ds(0, (nb - 1) * (FB // 2))], wos)
    drain(rfull.at[0], cs)
    if X > 2:
        drain(tall.at[0, back], tks.at[1])
        drain(tall.at[0, back], tks.at[4])
        drain(tall.at[0, front], tks.at[5])
        drain(tall.at[0, front], tks.at[2])
        drain(tall.at[0, back], tks.at[3])
        drain(lsend, lrs)
    elif X > 1:
        drain(lsend.at[0], lrs)
    if Y > 1:
        for q in (0, 1):
            drain(xall.at[pl.ds(0, Y - 1), quarters[q]], xs.at[4 + q])
        drain(precv.at[pl.ds(0, Y - 1)], oys)

    drain(rsum.at[pl.ds(0, Z - 1), 0], rs.at[0])

    @pl.when(c == 0)
    def _():
        drain(qbuf.at[0], qs)

    @pl.when(c == 1)
    def _():
        drain(rsum.at[pl.ds(0, Z - 1), 0], rs.at[1])
        for i in range(2):
            drain(kv.at[0, 0], kvs.at[i])
            drain(kv.at[0, 0, pl.ds(0, Z - 1)], kvs.at[i])

    @pl.when(owns)
    def _():
        drain(rsel.at[pl.ds(0, (Z - 1) * rz // slots)], ozs)

    @pl.when(jnp.logical_not(owns))
    def _():
        drain(rsel.at[pl.ds(0, Z * rz // slots)], ozs)


    @pl.when(keeps)
    def _():
        drain(rsel.at[pl.ds(0, S // 2 - 1)], rts)

    @pl.when(jnp.logical_not(keeps))
    def _():
        drain(rsel, rts)


def body(dims, tokens, light_input, light_output, heavy_input, heavy_output, query_tokens, context_tokens, query_gate):
    Z, Y, X = dims
    S = Z * Y * 2
    nb = 2 * Y
    slots = query_tokens.shape[1]
    T, FX = tokens.shape
    R = S * T // 32
    rz = R // Z
    D = light_input.shape[1]
    LX = light_input.shape[2]
    hbm = pl.BlockSpec(memory_space=pl.ANY)
    dma = pltpu.SemaphoreType.DMA
    scratch = [
        pltpu.VMEM((T, FX), BF),
        pltpu.VMEM(heavy_input.shape, BF),
        pltpu.VMEM((FB // 2, 2 * Y * HD), BF),
        pltpu.VMEM((slots, S), jnp.int32),
        pltpu.VMEM((slots, S), jnp.int32),
        pltpu.VMEM((1, slots), F32),
        pltpu.VMEM((Y, 2, 2, slots, FB), BF),
        pltpu.VMEM((Y // X, X, 2, 2, slots, FB), BF),
        pltpu.VMEM((S, slots, FB), BF),
        pltpu.VMEM((R, S * slots), BF),
        pltpu.VMEM((S * slots // 2, R), BF),
        pltpu.VMEM((Y, R, FB), BF),
        pltpu.VMEM((2, nb, FB // 2, 2 * HD), BF),
        pltpu.VMEM((Z, 2, rz, 2 * HD), BF),
        pltpu.VMEM((Z, 2, rz, 2 * HD), BF),
        pltpu.VMEM((2, 2, Z, rz, HD), BF),
        pltpu.VMEM((2, rz, HD), BF),
        pltpu.VMEM((rz, HD), BF),
        pltpu.VMEM((Z // 2 * rz, 2 * HD), BF),
        pltpu.VMEM((Y * FB, 2 * HD), BF),
        pltpu.VMEM((Y, Z // 2 * rz, FB), BF),
        pltpu.VMEM((Y, Z // 2 * rz, FB), BF),
        pltpu.VMEM((2, Z // 2 * rz, FB), BF),
        pltpu.VMEM((S // 2, slots, FB), BF),
        pltpu.VMEM((X, slots, FX), BF),
        pltpu.VMEM((X, T, FX), BF),
        pltpu.VMEM((3, D, LX), BF),
        pltpu.VMEM((LX, D), BF),
        pltpu.VMEM((3, T, LX), F32),
        pltpu.VMEM((T, LX), BF),
        pltpu.VMEM((3, T, FX), BF),
        pltpu.VMEM((2, T // 2, FX), BF),
        pltpu.VMEM((2, T, FX), BF),
        pltpu.VMEM((T, FX), F32),
        pltpu.VMEM((S * slots // 128, 128), F32),
        *[dma(()) for _ in range(21)],
        dma((6,)), dma((6,)), dma((8,)), dma((8,)), dma((2,)), dma((6,)),
        dma((2,)), dma((2,)), dma((2,)), dma((2,)), dma(()),
    ]
    return pl.pallas_call(
        functools.partial(kernel, dims),
        out_shape=jax.ShapeDtypeStruct((T, FX), BF),
        in_specs=[hbm] * 8,
        out_specs=pl.BlockSpec(memory_space=pltpu.VMEM),
        scratch_shapes=scratch,
        compiler_params=pltpu.CompilerParams(collective_id=0, has_side_effects=True, vmem_limit_bytes=48 << 20),
    )(*(
        pltpu.with_memory_space_constraint(a, pltpu.HBM)
        for a in (
            tokens, light_input, light_output, heavy_input, heavy_output.T, query_tokens.T, context_tokens.T, query_gate
        )
    ))


def solution(mesh):
    X = mesh.shape["head"]
    Z = 2 * X
    dims = (Z, mesh.shape["seq"] // (2 * Z), X)
    placed = (
        P("seq", "head"),
        P(None, None, "head"),
        P("head", None),
        P(None, "seq", "head"),
        P("head", "seq"),
        P(),
        P(),
        P("seq", None),
    )
    return jax.shard_map(
        functools.partial(body, dims), mesh=mesh, in_specs=placed, out_specs=P("seq", "head"), check_vma=False
    )
```
